32 devices in a mesh: rep: 2 (over x), ctx: 8 (over z, y), tp: 2 (over core).
Axes of the slice: x: 2, y: 2, z: 4, core: 2. Of those that a mesh axis runs over, the one named last changes fastest.
Arguments:
- queries: bfloat16 [4096, 4096], P(('rep', 'ctx'), 'tp'), parts along dimension 0, may hold values from -8 to 8
- rotated_key_rows: bfloat16 [4096, 512], P(('rep', 'ctx'), 'tp'), parts along dimension 0, may hold values from -8 to 8
- ordered_value_rows: bfloat16 [4096, 512], P(('rep', 'ctx'), 'tp'), parts along dimension 0, may hold values from -6 to 6
- block_order: int32 [32], P('rep'), parts along dimension 0, may hold values from 0 to 15, each once
- live_blocks: int32 [32, 12], P('rep'), parts along dimension 0, may hold values from -1 to 15, as said below
Outputs:
- attended: bfloat16 [4096, 4096], P(('rep', 'ctx', 'tp')), parts along dimension 0
- log_norm: float32 [64, 2048], P(('rep', 'tp'), 'ctx'), parts along dimension 0
The draws below stay inside these ranges and needn't reach their ends.
There are 2 independent parts, one for each index of `rep`. The reference program is written for one: setup_inputs(seed, part) draws one part's arguments, and reference() takes and returns one part's arrays. A program takes and returns all parts, laid end to end along the dimension named above; each array names one. Nothing has to cross between parts.
Inputs may be any that keep to these rules, and one draw needn't show every extreme that they name: `live_blocks`: row s names block s in its first slot, then distinct blocks before s, then -1 in every unused slot; row 15 fills all 12 slots.
All inputs are finite; a program needn't handle non-finite values.
Results may differ from the reference program's by a relative error of at most 0.008.
Values may be sent and summed in bfloat16 or wider, within the bound.
A program may use at most 128 MiB of HBM per device.

```python
import jax
import jax.numpy as jnp
from jax import lax

QUERY_HEADS = 32
KEY_VALUE_HEADS = 4
HEAD_SIZE = 128
BLOCK_TOKENS = 128
PROMPT_TOKENS = 2048
PROMPT_BLOCKS = 16
LIVE = 12


def base_random_field(key, shape):
    return jnp.clip(jax.random.normal(key, shape, jnp.float32), -8.0, 8.0)


def draw_queries(key, part):
    sampled_field = base_random_field(jax.random.fold_in(key, 1), (PROMPT_TOKENS, QUERY_HEADS * HEAD_SIZE))
    return sampled_field.astype(jnp.bfloat16)


def draw_rotated_key_rows(key, part):
    sampled_field = base_random_field(jax.random.fold_in(key, 2), (PROMPT_TOKENS, KEY_VALUE_HEADS * HEAD_SIZE))
    return sampled_field.astype(jnp.bfloat16)


def draw_live_blocks(key, part):
    first_key = jax.random.fold_in(key, 11)
    second_key = jax.random.fold_in(key, 12)
    row_ids = jnp.arange(PROMPT_BLOCKS, dtype=jnp.int32)
    uniform_pick = jax.random.randint(first_key, (PROMPT_BLOCKS,), 0, LIVE)
    wanted = LIVE - uniform_pick * uniform_pick // LIVE
    live_count = jnp.minimum(row_ids + 1, wanted)
    live_count = live_count.at[PROMPT_BLOCKS - 1].set(LIVE)
    col_ids = jnp.arange(PROMPT_BLOCKS, dtype=jnp.int32)
    ranked = jax.random.randint(second_key, (PROMPT_BLOCKS, PROMPT_BLOCKS), 0, 1 << 20) * PROMPT_BLOCKS + col_ids[None, :]
    ranked = jnp.where(col_ids[None, :] < row_ids[:, None], ranked, -1)
    top_values, earlier = jax.lax.top_k(ranked, LIVE - 1)
    slot_ids = jnp.arange(LIVE - 1, dtype=jnp.int32)
    entries = jnp.where(slot_ids[None, :] < live_count[:, None] - 1, earlier.astype(jnp.int32), -1)
    return jnp.concatenate([row_ids[:, None], entries], axis=1)


def block_levels(rng, dims, cuts, least, high):
    level = 1.0
    for dim, blocks in cuts:
        draws = jax.random.uniform(jax.random.fold_in(jax.random.fold_in(rng, 6), dim), (blocks,), jnp.float32, least / len(cuts), high / len(cuts))
        level = level * jnp.repeat(jnp.exp(draws), dims[dim] // blocks).reshape((-1,) + (1,) * (len(dims) - 1 - dim))
    return level


def scatter_about(stream_key, extent, deviation, reach, pieces=(), held_as=jnp.bfloat16):
    drawn = jax.random.normal(stream_key, extent, jnp.float32) * deviation
    if len(pieces) > 0:
        drawn = block_levels(stream_key, extent, pieces, -0.22, 0.18) * drawn
    return jnp.clip(drawn, min=-reach, max=reach).astype(held_as)


def setup_inputs(seed: int = 0, part: int = 0) -> dict:
    seeds = jax.random.split(jax.random.key(seed), 6)
    own_keys = jax.random.split(jax.random.fold_in(seeds[5], part), 6)
    return {
        "queries": draw_queries(jax.random.fold_in(jax.random.fold_in(seeds[5], part), 71), part),
        "rotated_key_rows": draw_rotated_key_rows(jax.random.fold_in(jax.random.fold_in(seeds[5], part), 71), part),
        "ordered_value_rows": scatter_about(own_keys[2], (PROMPT_TOKENS, KEY_VALUE_HEADS * HEAD_SIZE), 1.0, 6.0, ((0, 8), (1, 2))),
        "block_order": jax.random.permutation(own_keys[3], PROMPT_BLOCKS).astype(jnp.int32),
        "live_blocks": draw_live_blocks(jax.random.fold_in(jax.random.fold_in(seeds[5], part), 71), part),
    }


def reference(queries, rotated_key_rows, ordered_value_rows, block_order, live_blocks):
    query_groups = QUERY_HEADS // KEY_VALUE_HEADS
    factor = HEAD_SIZE ** -0.5
    block_ids = jnp.arange(PROMPT_BLOCKS, dtype=jnp.int32)
    inverse = jnp.zeros((PROMPT_BLOCKS,), jnp.int32).at[block_order].set(block_ids)
    blocked_keys = rotated_key_rows.reshape(PROMPT_BLOCKS, BLOCK_TOKENS, KEY_VALUE_HEADS, HEAD_SIZE)
    blocked_values = ordered_value_rows.reshape(PROMPT_BLOCKS, BLOCK_TOKENS, KEY_VALUE_HEADS, HEAD_SIZE)
    blocked_queries = queries.reshape(PROMPT_BLOCKS, BLOCK_TOKENS, KEY_VALUE_HEADS, query_groups, HEAD_SIZE)
    within = jnp.arange(BLOCK_TOKENS, dtype=jnp.int32)

    def one_block(index):
        seq_id = block_order[index]
        listed = live_blocks[seq_id]
        in_use = listed >= 0
        places = inverse[jnp.maximum(listed, 0)]
        picked_keys = blocked_keys[places].astype(jnp.float32)
        picked_values = blocked_values[places].astype(jnp.float32)
        query_part = blocked_queries[index].astype(jnp.float32)
        scores = jnp.einsum("qhgd,lkhd->hgqlk", query_part, picked_keys) * factor
        causal = within[None, None, :] <= within[:, None, None]
        allowed = in_use[None, :, None] & ((listed != seq_id)[None, :, None] | causal)
        scores = jnp.where(allowed, scores, -jnp.inf)
        row_peak = jnp.max(scores, axis=(3, 4))
        weights = jnp.where(allowed, jnp.exp(scores - row_peak[:, :, :, None, None]), 0.0)
        denominator = jnp.sum(weights, axis=(3, 4))
        rounded = lax.optimization_barrier(weights.astype(jnp.bfloat16)).astype(jnp.float32)
        summed = jnp.einsum("hgqlk,lkhd->hgqd", rounded, picked_values)
        normed = summed / denominator[..., None]
        merged_out = jnp.transpose(normed, (2, 0, 1, 3)).reshape(BLOCK_TOKENS, QUERY_HEADS * HEAD_SIZE).astype(jnp.bfloat16)
        norm_part = (row_peak + jnp.log(denominator)).reshape(QUERY_HEADS, BLOCK_TOKENS)
        return merged_out, norm_part

    out_blocks, norm_blocks = lax.map(one_block, block_ids)
    attended = out_blocks.reshape(PROMPT_TOKENS, QUERY_HEADS * HEAD_SIZE)
    log_norm = jnp.transpose(norm_blocks, (1, 0, 2)).reshape(QUERY_HEADS, PROMPT_TOKENS)
    return attended, log_norm
```

```python
import functools
import math

import jax
import jax.numpy as jnp
from jax import lax
from jax.experimental import pallas as pl
from jax.experimental.pallas import tpu as pltpu
from jax.sharding import PartitionSpec as P

HEAD_SIZE = 128
BLOCK_TOKENS = 128
CHUNK = 256
STRIP = 16
SLOTS = 4
FAR = 1e30
HUGE = 3e38
MESH = pl.DeviceIdType.MESH


def grid_of(count):
    minor = max(d for d in range(1, math.isqrt(count) + 1) if count % d == 0)
    return count // minor, minor


def kernel(
    dims,
    queries,
    keys,
    values,
    block_order,
    live_blocks,
    attended,
    log_norm,
    held,
    raw_queries,
    turned_queries,
    total,
    peak,
    weight_sum,
    leaving,
    limits,
    scores,
    load_sem,
    send_sem,
    recv_sem,
    swap_send,
    swap_recv,
):
    major, minor, tp_size, kv_local, groups, blocks_here, parts, slots_live = dims
    factor = HEAD_SIZE ** (-0.5)
    scale = factor * math.log2(math.e)
    width = groups * BLOCK_TOKENS
    per_part = blocks_here // parts
    me = lax.axis_index("ctx")
    mine = lax.axis_index("tp")
    a, b = me // minor, me % minor

    loads = {}
    for part in range(parts):
        for h in range(kv_local):
            for kb in range(per_part):
                at = pl.ds((part * per_part + kb) * BLOCK_TOKENS, BLOCK_TOKENS)
                lanes = pl.ds(h * HEAD_SIZE, HEAD_SIZE)
                for kind, source in enumerate((keys, values)):
                    loads[part, h, kb, kind] = pltpu.make_async_copy(
                        source.at[at, lanes],
                        held.at[me, part, h, kb, kind],
                        load_sem.at[part, h, kb, kind],
                    )
    for load in loads.values():
        load.start()
    load_queries = pltpu.make_async_copy(queries, raw_queries, load_sem.at[parts, 0, 0, 0])
    load_queries.start()

    barrier = pltpu.get_barrier_semaphore()
    sides = (
        (a > 0, me - minor),
        (a < major - 1, me + minor),
        (b > 0, me - 1),
        (b < minor - 1, me + 1),
    )
    for there, who in sides:

        @pl.when(there)
        def _(who=who):
            pl.semaphore_signal(barrier, inc=1, device_id={"ctx": who}, device_id_type=MESH)

    for turn in range(1, tp_size):
        peer = (mine + turn) % tp_size
        pl.semaphore_signal(barrier, inc=1, device_id={"tp": peer}, device_id_type=MESH)
    expected = jnp.int32(tp_size - 1)
    for there, _ in sides:
        expected = expected + there.astype(jnp.int32)
    pl.semaphore_wait(barrier, expected)

    def onward(part, i, j):
        column_first = j == b
        row_first = (i == 0) | (i == major - 1) if part == parts - 1 and parts > 1 else jnp.bool_(False)
        along = column_first | row_first
        across = (i == a) | jnp.logical_not(row_first)
        return (
            (i >= a) & (a > 0) & along,
            (i <= a) & (a < major - 1) & along,
            (j >= b) & (b > 0) & across,
            (j <= b) & (b < minor - 1) & across,
        )

    def send_on(slot, part, h, i, j):
        for side, wanted in enumerate(onward(part, i, j)):

            @pl.when(wanted)
            def _(side=side):
                pltpu.make_async_remote_copy(
                    src_ref=held.at[slot, part, h],
                    dst_ref=held.at[slot, part, h],
                    send_sem=send_sem.at[slot, part, side],
                    recv_sem=recv_sem.at[slot, part, h],
                    device_id={"ctx": sides[side][1]},
                    device_id_type=MESH,
                ).start()

    def settle(slot, i, j):
        for part in range(parts):
            for side, wanted in enumerate(onward(part, i, j)):

                @pl.when(wanted)
                def _(part=part, side=side):
                    pltpu.make_async_copy(
                        held.at[slot, part], held.at[slot, part], send_sem.at[slot, part, side]
                    ).wait()

    def find_limits(slot):
        for query_block in range(blocks_here):
            my_seq = block_order[0, me * blocks_here + query_block]
            found = [jnp.bool_(False)] * blocks_here
            names = [block_order[0, slot * blocks_here + kb] for kb in range(blocks_here)]
            for entry in range(slots_live):
                listed = live_blocks[my_seq, entry]
                found = [f | (listed == name) for f, name in zip(found, names)]
            for kb in range(blocks_here):
                limits[0, query_block * blocks_here + kb] = jnp.where(found[kb], HUGE, -FAR)
                limits[1, query_block * blocks_here + kb] = jnp.where(found[kb], -HUGE, FAR)

    def attend(slot, h, own):
        units = [
            (query_block, start)
            for query_block in range(blocks_here)
            for start in range(0, width, CHUNK)
        ]
        blocks = [(kb // per_part, kb % per_part) for kb in range(blocks_here)]
        keys_here = jnp.concatenate([held[slot, part, h, kb, 0] for part, kb in blocks], axis=0)
        turned_values = jnp.transpose(
            jnp.concatenate([held[slot, part, h, kb, 1] for part, kb in blocks], axis=0)
        )

        def score(u):
            query_block, start = units[u]
            part = jnp.dot(
                keys_here,
                turned_queries[query_block, h, :, pl.ds(start, CHUNK)],
                preferred_element_type=jnp.float32,
            )
            tops = []
            for kb in range(blocks_here):
                block = part[kb * BLOCK_TOKENS : (kb + 1) * BLOCK_TOKENS]
                if own and kb == query_block:
                    key_at = lax.broadcasted_iota(jnp.int32, block.shape, 0)
                    row_at = lax.broadcasted_iota(jnp.int32, block.shape, 1) % BLOCK_TOKENS
                    block = jnp.where(key_at <= row_at, block, -FAR)
                scores[u % SLOTS, pl.ds(kb * BLOCK_TOKENS, BLOCK_TOKENS), :] = block
                tops.append(jnp.max(block, axis=0, keepdims=True))
            return tops

        def absorb(u, tops):
            query_block, start = units[u]
            lanes = pl.ds(start, CHUNK)
            first = query_block * blocks_here
            new_peak = None
            for kb, top in enumerate(tops):
                top = jnp.minimum(top, limits[0, first + kb])
                new_peak = top if new_peak is None else jnp.maximum(new_peak, top)
            if not own:
                old_peak = peak[query_block, h, :, lanes]
                new_peak = jnp.maximum(new_peak, old_peak)
            peak[query_block, h, :, lanes] = new_peak
            level = new_peak * scale
            added = None
            low = []
            for kb in range(blocks_here):
                floor = jnp.maximum(level, limits[1, first + kb])
                for at in range(kb * BLOCK_TOKENS, (kb + 1) * BLOCK_TOKENS, STRIP):
                    w = jnp.exp2(scores[u % SLOTS, pl.ds(at, STRIP), :] * scale - floor)
                    added = w if added is None else added + w
                    low.append(w.astype(jnp.bfloat16))
            added = jnp.sum(added, axis=0, keepdims=True)
            product = jnp.dot(
                turned_values,
                jnp.concatenate(low, axis=0),
                preferred_element_type=jnp.float32,
            )
            if own:
                weight_sum[query_block, h, :, lanes] = added
                total[query_block, h, :, lanes] = product
            else:
                fade = jnp.exp2((old_peak - new_peak) * scale)
                weight_sum[query_block, h, :, lanes] = (
                    weight_sum[query_block, h, :, lanes] * fade + added
                )
                total[query_block, h, :, lanes] = total[query_block, h, :, lanes] * fade + product

        waiting = [score(u) for u in range(SLOTS - 1)]
        for u in range(len(units)):
            if u + SLOTS - 1 < len(units):
                waiting.append(score(u + SLOTS - 1))
            absorb(u, waiting[u])

    per_peer = blocks_here // tp_size
    wide = kv_local * width

    def swap(turn, k, h):
        peer = (mine + turn) % tp_size
        source = pl.ds(h * width, width)
        target = pl.ds(pl.multiple_of(mine * wide + h * width, HEAD_SIZE), width)
        return pltpu.make_async_remote_copy(
            src_ref=leaving.at[peer * per_peer + k, :, source],
            dst_ref=attended.at[pl.ds(k * BLOCK_TOKENS, BLOCK_TOKENS), target],
            send_sem=swap_send.at[turn - 1, k, h],
            recv_sem=swap_recv.at[turn - 1, k, h],
            device_id={"tp": peer},
            device_id_type=MESH,
        )

    def finish(h):
        for turn in range(1, tp_size + 1):
            peer = (mine + turn) % tp_size
            for k in range(per_peer):
                query_block = peer * per_peer + k
                at = pl.ds(pl.multiple_of(query_block * BLOCK_TOKENS, BLOCK_TOKENS), BLOCK_TOKENS)
                for g in range(groups):
                    head = h * groups + g
                    lanes = pl.ds(g * BLOCK_TOKENS, BLOCK_TOKENS)
                    bottom = weight_sum[query_block, h, :, lanes]
                    normed = total[query_block, h, :, lanes] * (1.0 / bottom)
                    tile = jnp.transpose(normed.astype(jnp.bfloat16))
                    if turn < tp_size:
                        leaving[query_block, :, pl.ds(head * HEAD_SIZE, HEAD_SIZE)] = tile
                    else:
                        to = pl.multiple_of(mine * wide + head * HEAD_SIZE, HEAD_SIZE)
                        attended[pl.ds(k * BLOCK_TOKENS, BLOCK_TOKENS), pl.ds(to, HEAD_SIZE)] = tile
                    log_norm[pl.ds(head, 1), at] = (
                        peak[query_block, h, :, lanes] * factor + jnp.log(bottom)
                    )
                if turn < tp_size:
                    swap(turn, k, h).start()

    for part in range(parts):
        for h in range(kv_local):
            for kb in range(per_part):
                for kind in range(2):
                    loads[part, h, kb, kind].wait()
    for h in range(kv_local):
        for part in range(parts):
            send_on(me, part, h, a, b)
    load_queries.wait()

    def turn_block(query_block, carry):
        at = pl.ds(pl.multiple_of(query_block * BLOCK_TOKENS, BLOCK_TOKENS), BLOCK_TOKENS)
        for h in range(kv_local):
            for g in range(groups):
                head = h * groups + g
                turned_queries[query_block, h, :, pl.ds(g * BLOCK_TOKENS, BLOCK_TOKENS)] = (
                    jnp.transpose(raw_queries[at, pl.ds(head * HEAD_SIZE, HEAD_SIZE)])
                )
        return carry

    lax.fori_loop(0, blocks_here, turn_block, 0)
    find_limits(me)
    for h in range(kv_local):
        attend(me, h, True)

    def nearest(x, n, k):
        both = jnp.minimum(x, n - 1 - x)
        away = 1 - 2 * (2 * x > n - 1).astype(jnp.int32)
        paired = ((k + 1) // 2) * (2 * (k % 2) - 1)
        return x + away * jnp.where(k <= 2 * both, paired, k - both)

    lag = 1 + ((a > 0) & (a < major - 1)).astype(jnp.int32)

    def place_of(turn):
        l = turn % minor
        k = turn // minor - lag * l
        fits = (k >= 0) & (k < major)
        return fits, k, l, nearest(a, major, k), nearest(b, minor, l)

    rounds = (major + 2 * (minor - 1)) * minor

    def one_shard(turn, carry):
        fits, k, l, i, j = place_of(turn)
        slot = i * minor + j
        last = (k == major - 1) & (l == minor - 1)

        @pl.when(fits & (k + l > 0))
        def _():
            @pl.when(last)
            def _():
                lax.fori_loop(0, rounds, settle_early, 0)

            find_limits(slot)
            for h in range(kv_local):
                for part in range(parts):
                    pltpu.make_async_copy(
                        held.at[slot, part, h], held.at[slot, part, h], recv_sem.at[slot, part, h]
                    ).wait()
                    send_on(slot, part, h, i, j)
                attend(slot, h, False)

                @pl.when(last)
                def _(h=h):
                    finish(h)

        return carry

    def settle_early(turn, carry):
        fits, k, l, i, j = place_of(turn)

        @pl.when(fits & (k < major - 1))
        def _():
            settle(i * minor + j, i, j)

        return carry

    def settle_late(l, carry):
        i, j = nearest(a, major, jnp.int32(major - 1)), nearest(b, minor, l)
        settle(i * minor + j, i, j)
        return carry

    lax.fori_loop(0, rounds, one_shard, 0)
    lax.fori_loop(0, minor, settle_late, 0)
    for turn in range(1, tp_size):
        for k in range(per_peer):
            for h in range(kv_local):
                swap(turn, k, h).wait()


def copy_out(attended, log_norm, attended_out, log_norm_out, sems):
    copies = [
        pltpu.make_async_copy(log_norm, log_norm_out, sems.at[0]),
        pltpu.make_async_copy(attended, attended_out, sems.at[1]),
    ]
    for copy in copies:
        copy.start()
    for copy in copies:
        copy.wait()


def body(tp_size, ctx_size, queries, rotated_key_rows, ordered_value_rows, block_order, live_blocks):
    tok_rows, own_columns = queries.shape
    kv_columns = rotated_key_rows.shape[1]
    kv_local = kv_columns // HEAD_SIZE
    heads_local = own_columns // HEAD_SIZE
    groups = heads_local // kv_local
    blocks_here = tok_rows // BLOCK_TOKENS
    width = groups * BLOCK_TOKENS
    major, minor = grid_of(ctx_size)
    parts = 2 if blocks_here % 2 == 0 else 1
    dims = (major, minor, tp_size, kv_local, groups, blocks_here, parts, live_blocks.shape[1])
    per_peer = blocks_here // tp_size
    per_part = blocks_here // parts
    whole = pl.BlockSpec(memory_space=pltpu.VMEM)
    small = pl.BlockSpec(memory_space=pltpu.SMEM)
    apart = pl.BlockSpec(memory_space=pl.ANY)
    attended, log_norm = pl.pallas_call(
        functools.partial(kernel, dims),
        out_shape=(
            pltpu.VMEM((tok_rows // tp_size, own_columns * tp_size), jnp.bfloat16),
            pltpu.VMEM((heads_local, tok_rows), jnp.float32),
        ),
        in_specs=[apart, apart, apart, small, small],
        out_specs=(whole, whole),
        scratch_shapes=[
            pltpu.VMEM(
                (ctx_size, parts, kv_local, per_part, 2, BLOCK_TOKENS, HEAD_SIZE), jnp.bfloat16
            ),
            pltpu.VMEM((tok_rows, own_columns), jnp.bfloat16),
            pltpu.VMEM((blocks_here, kv_local, HEAD_SIZE, width), jnp.bfloat16),
            pltpu.VMEM((blocks_here, kv_local, HEAD_SIZE, width), jnp.float32),
            pltpu.VMEM((blocks_here, kv_local, 1, width), jnp.float32),
            pltpu.VMEM((blocks_here, kv_local, 1, width), jnp.float32),
            pltpu.VMEM((blocks_here, BLOCK_TOKENS, own_columns), jnp.bfloat16),
            pltpu.SMEM((2, blocks_here * blocks_here), jnp.float32),
            pltpu.VMEM((SLOTS, tok_rows, CHUNK), jnp.float32),
            pltpu.SemaphoreType.DMA((parts + 1, kv_local, per_part, 2)),
            pltpu.SemaphoreType.DMA((ctx_size, parts, 4)),
            pltpu.SemaphoreType.DMA((ctx_size, parts, kv_local)),
            pltpu.SemaphoreType.DMA((tp_size - 1, per_peer, kv_local)),
            pltpu.SemaphoreType.DMA((tp_size - 1, per_peer, kv_local)),
        ],
        compiler_params=pltpu.CompilerParams(collective_id=0, has_side_effects=True),
        name="gather_attend",
    )(queries, rotated_key_rows, ordered_value_rows, block_order.reshape(1, -1), live_blocks)
    return pl.pallas_call(
        copy_out,
        out_shape=(
            jax.ShapeDtypeStruct(attended.shape, attended.dtype),
            jax.ShapeDtypeStruct(log_norm.shape, log_norm.dtype),
        ),
        in_specs=[whole, whole],
        out_specs=(apart, apart),
        scratch_shapes=[pltpu.SemaphoreType.DMA((2,))],
        name="copy_out",
    )(
        pltpu.with_memory_space_constraint(attended, pltpu.VMEM),
        pltpu.with_memory_space_constraint(log_norm, pltpu.VMEM),
    )


def solution(mesh):
    placed = (
        P(("rep", "ctx"), "tp"),
        P(("rep", "ctx"), "tp"),
        P(("rep", "ctx"), "tp"),
        P("rep"),
        P("rep", None),
    )
    return jax.shard_map(
        functools.partial(body, mesh.shape["tp"], mesh.shape["ctx"]),
        mesh=mesh,
        in_specs=placed,
        out_specs=(P(("rep", "ctx", "tp"), None), P(("rep", "tp"), "ctx")),
        check_vma=False,
    )
```

```python
import functools
import math

import jax
import jax.numpy as jnp
from jax import lax
from jax.experimental import pallas as pl
from jax.experimental.pallas import tpu as pltpu
from jax.sharding import PartitionSpec as P

HEAD_SIZE = 128
BLOCK_TOKENS = 128
CHUNK = 256
STRIP = 16
SLOTS = 4
FAR = 1e30
HUGE = 3e38
MESH = pl.DeviceIdType.MESH


def grid_of(count):
    minor = max(d for d in range(1, math.isqrt(count) + 1) if count % d == 0)
    return count // minor, minor


def kernel(
    dims,
    queries,
    keys,
    values,
    block_order,
    live_blocks,
    attended,
    log_norm,
    held,
    own,
    order,
    live,
    raw_queries,
    turned_queries,
    total,
    peak,
    weight_sum,
    leaving,
    limits,
    scores,
    load_sem,
    send_sem,
    recv_sem,
    swap_send,
    swap_recv,
):
    major, minor, tp_size, kv_local, groups, blocks_here, parts, slots_live = dims
    factor = HEAD_SIZE ** (-0.5)
    scale = factor * math.log2(math.e)
    width = groups * BLOCK_TOKENS
    per_part = blocks_here // parts
    me = lax.axis_index("ctx")
    mine = lax.axis_index("tp")
    a, b = me // minor, me % minor

    tables = [
        pltpu.make_async_copy(block_order, order, load_sem.at[0]),
        pltpu.make_async_copy(live_blocks, live, load_sem.at[1]),
    ]
    loads = [
        pltpu.make_async_copy(keys, own.at[0], load_sem.at[2]),
        pltpu.make_async_copy(values, own.at[1], load_sem.at[3]),
        pltpu.make_async_copy(queries, raw_queries, load_sem.at[4]),
    ]
    barrier = pltpu.get_barrier_semaphore()
    sides = (
        (a > 0, me - minor),
        (a < major - 1, me + minor),
        (b > 0, me - 1),
        (b < minor - 1, me + 1),
    )
    for there, who in sides:

        @pl.when(there)
        def _(who=who):
            pl.semaphore_signal(barrier, inc=1, device_id={"ctx": who}, device_id_type=MESH)

    for turn in range(1, tp_size):
        peer = (mine + turn) % tp_size
        pl.semaphore_signal(barrier, inc=1, device_id={"tp": peer}, device_id_type=MESH)
    for load in tables + loads:
        load.start()
    expected = jnp.int32(tp_size - 1)
    for there, _ in sides:
        expected = expected + there.astype(jnp.int32)
    pl.semaphore_wait(barrier, expected)

    def onward(part, i, j):
        column_first = j == b
        row_first = (i == 0) | (i == major - 1) if part == parts - 1 and parts > 1 else jnp.bool_(False)
        along = column_first | row_first
        across = (i == a) | jnp.logical_not(row_first)
        return (
            (i >= a) & (a > 0) & along,
            (i <= a) & (a < major - 1) & along,
            (j >= b) & (b > 0) & across,
            (j <= b) & (b < minor - 1) & across,
        )

    def send_on(slot, part, h, i, j):
        for side, wanted in enumerate(onward(part, i, j)):

            @pl.when(wanted)
            def _(side=side):
                pltpu.make_async_remote_copy(
                    src_ref=held.at[slot, part, h],
                    dst_ref=held.at[slot, part, h],
                    send_sem=send_sem.at[slot, part, side],
                    recv_sem=recv_sem.at[slot, part, h],
                    device_id={"ctx": sides[side][1]},
                    device_id_type=MESH,
                ).start()

    def send_own(part, h):
        for side, wanted in enumerate(onward(part, a, b)):

            @pl.when(wanted)
            def _(side=side):
                for kb in range(per_part):
                    at = pl.ds((part * per_part + kb) * BLOCK_TOKENS, BLOCK_TOKENS)
                    for kind, source in enumerate((keys, values)):
                        pltpu.make_async_remote_copy(
                            src_ref=source.at[at, pl.ds(h * HEAD_SIZE, HEAD_SIZE)],
                            dst_ref=held.at[me, part, h, kb, kind],
                            send_sem=send_sem.at[me, part, side],
                            recv_sem=recv_sem.at[me, part, h],
                            device_id={"ctx": sides[side][1]},
                            device_id_type=MESH,
                        ).start()

    def settle(slot, i, j):
        for part in range(parts):
            for side, wanted in enumerate(onward(part, i, j)):

                @pl.when(wanted)
                def _(part=part, side=side):
                    pltpu.make_async_copy(
                        held.at[slot, part], held.at[slot, part], send_sem.at[slot, part, side]
                    ).wait()

    def find_limits(slot, carry):
        for query_block in range(blocks_here):
            my_seq = order[0, me * blocks_here + query_block]
            found = [jnp.bool_(False)] * blocks_here
            names = [order[0, slot * blocks_here + kb] for kb in range(blocks_here)]
            for entry in range(slots_live):
                listed = live[my_seq, entry]
                found = [f | (listed == name) for f, name in zip(found, names)]
            for kb in range(blocks_here):
                limits[slot, query_block, kb] = jnp.where(found[kb], HUGE, -FAR)
        return carry

    def attend(slot, h, first, after=None):
        if first:
            lanes = pl.ds(pl.multiple_of(h * HEAD_SIZE, HEAD_SIZE), HEAD_SIZE)
            keys_here, values_here = own[0, :, lanes], own[1, :, lanes]
        else:
            blocks = [(kb // per_part, kb % per_part) for kb in range(blocks_here)]
            keys_here, values_here = (
                jnp.concatenate([held[slot, part, h, kb, kind] for part, kb in blocks], axis=0)
                for kind in range(2)
            )
        turned_values = jnp.transpose(values_here)
        turned = (mine + 1) * per_peer
        units = [
            (q if first else (turned + q) % blocks_here, q, start)
            for q in range(blocks_here)
            for start in range(0, width, CHUNK)
        ]

        def score(u):
            query_block, q, start = units[u]
            part = jnp.dot(
                keys_here,
                turned_queries[query_block, h, :, pl.ds(start, CHUNK)],
                preferred_element_type=jnp.float32,
            )
            tops = []
            for kb in range(blocks_here):
                block = part[kb * BLOCK_TOKENS : (kb + 1) * BLOCK_TOKENS]
                if first and kb == q:
                    key_at = lax.broadcasted_iota(jnp.int32, block.shape, 0)
                    row_at = lax.broadcasted_iota(jnp.int32, block.shape, 1) % BLOCK_TOKENS
                    block = jnp.where(key_at <= row_at, block, -FAR)
                scores[u % SLOTS, pl.ds(kb * BLOCK_TOKENS, BLOCK_TOKENS), :] = block
                tops.append(jnp.max(block, axis=0, keepdims=True))
            return tops

        def absorb(u, tops):
            query_block, q, start = units[u]
            lanes = pl.ds(start, CHUNK)
            new_peak = None
            for kb, top in enumerate(tops):
                top = jnp.minimum(top, limits[slot, query_block, kb])
                new_peak = top if new_peak is None else jnp.maximum(new_peak, top)
            if not first:
                old_peak = peak[query_block, h, :, lanes]
                new_peak = jnp.maximum(new_peak, old_peak)
            peak[query_block, h, :, lanes] = new_peak
            level = new_peak * scale
            added = None
            low = []
            for kb in range(blocks_here):
                floor = jnp.maximum(level, -limits[slot, query_block, kb])
                for at in range(kb * BLOCK_TOKENS, (kb + 1) * BLOCK_TOKENS, STRIP):
                    w = jnp.exp2(scores[u % SLOTS, pl.ds(at, STRIP), :] * scale - floor)
                    added = w if added is None else added + w
                    low.append(w.astype(jnp.bfloat16))
            added = jnp.sum(added, axis=0, keepdims=True)
            product = jnp.dot(
                turned_values,
                jnp.concatenate(low, axis=0),
                preferred_element_type=jnp.float32,
            )
            if first:
                weight_sum[query_block, h, :, lanes] = added
                total[query_block, h, :, lanes] = product
            else:
                fade = jnp.exp2((old_peak - new_peak) * scale)
                weight_sum[query_block, h, :, lanes] = (
                    weight_sum[query_block, h, :, lanes] * fade + added
                )
                total[query_block, h, :, lanes] = total[query_block, h, :, lanes] * fade + product

        waiting = [score(u) for u in range(SLOTS - 1)]
        for u in range(len(units)):
            if u + SLOTS - 1 < len(units):
                waiting.append(score(u + SLOTS - 1))
            absorb(u, waiting[u])
            if after is not None and (u + 1) % (len(units) // blocks_here) == 0:
                after(units[u][1])

    per_peer = blocks_here // tp_size
    wide = kv_local * width

    def swap(turn, k, h):
        peer = (mine + turn) % tp_size
        source = pl.ds(pl.multiple_of(h * width, HEAD_SIZE), width)
        target = pl.ds(pl.multiple_of(mine * wide + h * width, HEAD_SIZE), width)
        return pltpu.make_async_remote_copy(
            src_ref=leaving.at[peer * per_peer + k, :, source],
            dst_ref=attended.at[pl.ds(k * BLOCK_TOKENS, BLOCK_TOKENS), target],
            send_sem=swap_send.at[turn - 1, k, h],
            recv_sem=swap_recv.at[turn - 1, k, h],
            device_id={"tp": peer},
            device_id_type=MESH,
        )

    def finish(h, q):
        turn, k = 1 + q // per_peer, q % per_peer
        peer = (mine + turn) % tp_size
        query_block = peer * per_peer + k
        at = pl.ds(pl.multiple_of(query_block * BLOCK_TOKENS, BLOCK_TOKENS), BLOCK_TOKENS)
        norms = []
        for g in range(groups):
            head = h * groups + g
            lanes = pl.ds(g * BLOCK_TOKENS, BLOCK_TOKENS)
            bottom = weight_sum[query_block, h, :, lanes]
            normed = total[query_block, h, :, lanes] * (1.0 / bottom)
            tile = jnp.transpose(normed.astype(jnp.bfloat16))
            if turn < tp_size:
                to = pl.multiple_of(head * HEAD_SIZE, HEAD_SIZE)
                leaving[query_block, :, pl.ds(to, HEAD_SIZE)] = tile
            else:
                to = pl.multiple_of(mine * wide + head * HEAD_SIZE, HEAD_SIZE)
                attended[pl.ds(k * BLOCK_TOKENS, BLOCK_TOKENS), pl.ds(to, HEAD_SIZE)] = tile
            norms.append(peak[query_block, h, :, lanes] * factor + jnp.log(bottom))
        heads = pl.ds(pl.multiple_of(h * groups, groups), groups)
        log_norm[heads, at] = jnp.concatenate(norms, axis=0)
        if turn < tp_size:
            swap(turn, k, h).start()

    for h in range(kv_local):
        for part in range(parts):
            send_own(part, h)
    for load in tables + loads:
        load.wait()

    def turn_block(query_block, carry):
        at = pl.ds(pl.multiple_of(query_block * BLOCK_TOKENS, BLOCK_TOKENS), BLOCK_TOKENS)
        for h in range(kv_local):
            for g in range(groups):
                head = h * groups + g
                turned_queries[query_block, h, :, pl.ds(g * BLOCK_TOKENS, BLOCK_TOKENS)] = (
                    jnp.transpose(raw_queries[at, pl.ds(head * HEAD_SIZE, HEAD_SIZE)])
                )
        return carry

    lax.fori_loop(0, blocks_here, turn_block, 0)
    lax.fori_loop(me, me + 1, find_limits, 0)

    def attend_own(h, carry):
        attend(me, h, True)
        return carry

    lax.fori_loop(0, kv_local, attend_own, 0)
    lax.fori_loop(0, major * minor, find_limits, 0)

    def nearest(x, n, k):
        both = jnp.minimum(x, n - 1 - x)
        away = 1 - 2 * (2 * x > n - 1).astype(jnp.int32)
        paired = ((k + 1) // 2) * (2 * (k % 2) - 1)
        return x + away * jnp.where(k <= 2 * both, paired, k - both)

    lag = 1 + ((a > 0) & (a < major - 1)).astype(jnp.int32)
    waves = major - 1 + lag * (minor - 1)

    def place_of(wave, l):
        k = wave - lag * l
        return (k >= 0) & (k < major), k, nearest(a, major, k), nearest(b, minor, l)

    def take(slot, h, i, j):
        for part in range(parts):
            pltpu.make_async_copy(
                held.at[slot, part, h], held.at[slot, part, h], recv_sem.at[slot, part, h]
            ).wait()
            send_on(slot, part, h, i, j)

    def one_turn(turn, carry):
        l, h = turn % minor, (turn // minor) % kv_local
        fits, k, i, j = place_of(turn // (minor * kv_local), l)
        slot = i * minor + j

        @pl.when(fits & (k + l > 0))
        def _():
            take(slot, h, i, j)
            attend(slot, h, False)

        return carry

    lax.fori_loop(kv_local * minor, waves * kv_local * minor, one_turn, 0)

    def settle_one(turn, carry):
        fits, _, i, j = place_of(turn // minor, turn % minor)

        @pl.when(fits)
        def _():
            settle(i * minor + j, i, j)

        return carry

    early = (waves - lag) * minor
    lax.fori_loop(0, early, settle_one, 0)
    far_i, far_j = nearest(a, major, jnp.int32(major - 1)), nearest(b, minor, jnp.int32(minor - 1))

    def last_turn(h, carry):
        slot = far_i * minor + far_j
        take(slot, h, far_i, far_j)
        attend(slot, h, False, functools.partial(finish, h))
        return carry

    lax.fori_loop(0, kv_local, last_turn, 0)
    lax.fori_loop(early, (waves + 1) * minor, settle_one, 0)
    for turn in range(1, tp_size):
        for k in range(per_peer):
            for h in range(kv_local):
                swap(turn, k, h).wait()


def copy_out(attended, log_norm, attended_out, log_norm_out, sems):
    copies = [
        pltpu.make_async_copy(log_norm, log_norm_out, sems.at[0]),
        pltpu.make_async_copy(attended, attended_out, sems.at[1]),
    ]
    for copy in copies:
        copy.start()
    for copy in copies:
        copy.wait()


def body(tp_size, ctx_size, queries, rotated_key_rows, ordered_value_rows, block_order, live_blocks):
    tok_rows, own_columns = queries.shape
    kv_columns = rotated_key_rows.shape[1]
    kv_local = kv_columns // HEAD_SIZE
    heads_local = own_columns // HEAD_SIZE
    groups = heads_local // kv_local
    blocks_here = tok_rows // BLOCK_TOKENS
    width = groups * BLOCK_TOKENS
    major, minor = grid_of(ctx_size)
    parts = 2 if blocks_here % 2 == 0 else 1
    dims = (major, minor, tp_size, kv_local, groups, blocks_here, parts, live_blocks.shape[1])
    per_peer = blocks_here // tp_size
    per_part = blocks_here // parts
    whole = pl.BlockSpec(memory_space=pltpu.VMEM)
    apart = pl.BlockSpec(memory_space=pl.ANY)
    attended, log_norm = pl.pallas_call(
        functools.partial(kernel, dims),
        out_shape=(
            pltpu.VMEM((tok_rows // tp_size, own_columns * tp_size), jnp.bfloat16),
            pltpu.VMEM((heads_local, tok_rows), jnp.float32),
        ),
        in_specs=[apart] * 5,
        out_specs=(whole, whole),
        scratch_shapes=[
            pltpu.VMEM(
                (ctx_size, parts, kv_local, per_part, 2, BLOCK_TOKENS, HEAD_SIZE), jnp.bfloat16
            ),
            pltpu.VMEM((2, tok_rows, kv_columns), jnp.bfloat16),
            pltpu.SMEM((1, block_order.shape[0]), jnp.int32),
            pltpu.SMEM(live_blocks.shape, jnp.int32),
            pltpu.VMEM((tok_rows, own_columns), jnp.bfloat16),
            pltpu.VMEM((blocks_here, kv_local, HEAD_SIZE, width), jnp.bfloat16),
            pltpu.VMEM((blocks_here, kv_local, HEAD_SIZE, width), jnp.float32),
            pltpu.VMEM((blocks_here, kv_local, 1, width), jnp.float32),
            pltpu.VMEM((blocks_here, kv_local, 1, width), jnp.float32),
            pltpu.VMEM((blocks_here, BLOCK_TOKENS, own_columns), jnp.bfloat16),
            pltpu.SMEM((ctx_size, blocks_here, blocks_here), jnp.float32),
            pltpu.VMEM((SLOTS, tok_rows, CHUNK), jnp.float32),
            pltpu.SemaphoreType.DMA((5,)),
            pltpu.SemaphoreType.DMA((ctx_size, parts, 4)),
            pltpu.SemaphoreType.DMA((ctx_size, parts, kv_local)),
            pltpu.SemaphoreType.DMA((tp_size - 1, per_peer, kv_local)),
            pltpu.SemaphoreType.DMA((tp_size - 1, per_peer, kv_local)),
        ],
        compiler_params=pltpu.CompilerParams(collective_id=0, has_side_effects=True),
        name="gather_attend",
    )(queries, rotated_key_rows, ordered_value_rows, block_order.reshape(1, -1), live_blocks)
    return pl.pallas_call(
        copy_out,
        out_shape=(
            jax.ShapeDtypeStruct(attended.shape, attended.dtype),
            jax.ShapeDtypeStruct(log_norm.shape, log_norm.dtype),
        ),
        in_specs=[whole, whole],
        out_specs=(apart, apart),
        scratch_shapes=[pltpu.SemaphoreType.DMA((2,))],
        name="copy_out",
    )(
        pltpu.with_memory_space_constraint(attended, pltpu.VMEM),
        pltpu.with_memory_space_constraint(log_norm, pltpu.VMEM),
    )


def solution(mesh):
    placed = (
        P(("rep", "ctx"), "tp"),
        P(("rep", "ctx"), "tp"),
        P(("rep", "ctx"), "tp"),
        P("rep"),
        P("rep", None),
    )
    return jax.shard_map(
        functools.partial(body, mesh.shape["tp"], mesh.shape["ctx"]),
        mesh=mesh,
        in_specs=placed,
        out_specs=(P(("rep", "ctx", "tp"), None), P(("rep", "tp"), "ctx")),
        check_vma=False,
    )
```

```python
import functools
import math

import jax
import jax.numpy as jnp
from jax import lax
from jax.experimental import pallas as pl
from jax.experimental.pallas import tpu as pltpu
from jax.sharding import PartitionSpec as P

HEAD_SIZE = 128
BLOCK_TOKENS = 128
CHUNK = 256
STRIP = 16
SLOTS = 4
FAR = 1e30
HUGE = 3e38
MESH = pl.DeviceIdType.MESH


def grid_of(count):
    minor = max(d for d in range(1, math.isqrt(count) + 1) if count % d == 0)
    return count // minor, minor


def kernel(
    dims,
    queries,
    keys,
    values,
    block_order,
    live_blocks,
    attended,
    log_norm,
    held,
    own,
    order,
    live,
    raw_queries,
    turned_queries,
    total,
    peak,
    weight_sum,
    leaving,
    limits,
    scores,
    load_sem,
    send_sem,
    recv_sem,
    swap_send,
    swap_recv,
):
    major, minor, tp_size, kv_local, groups, blocks_here, cut, slots_live = dims
    factor = HEAD_SIZE ** (-0.5)
    scale = factor * math.log2(math.e)
    width = groups * BLOCK_TOKENS
    rows = blocks_here * BLOCK_TOKENS
    spans = [pl.ds(0, cut), pl.ds(cut, rows - cut)]
    parts = len(spans)
    me = lax.axis_index("ctx")
    mine = lax.axis_index("tp")
    a, b = me // minor, me % minor

    tables = [
        pltpu.make_async_copy(block_order, order, load_sem.at[0]),
        pltpu.make_async_copy(live_blocks, live, load_sem.at[1]),
    ]
    loads = [
        pltpu.make_async_copy(keys, own.at[0], load_sem.at[2]),
        pltpu.make_async_copy(values, own.at[1], load_sem.at[3]),
        pltpu.make_async_copy(queries, raw_queries, load_sem.at[4]),
    ]
    barrier = pltpu.get_barrier_semaphore()
    sides = (
        (a > 0, me - minor),
        (a < major - 1, me + minor),
        (b > 0, me - 1),
        (b < minor - 1, me + 1),
    )
    for there, who in sides:

        @pl.when(there)
        def _(who=who):
            pl.semaphore_signal(barrier, inc=1, device_id={"ctx": who}, device_id_type=MESH)

    for turn in range(1, tp_size):
        peer = (mine + turn) % tp_size
        pl.semaphore_signal(barrier, inc=1, device_id={"tp": peer}, device_id_type=MESH)
    for load in tables + loads:
        load.start()
    expected = jnp.int32(tp_size - 1)
    for there, _ in sides:
        expected = expected + there.astype(jnp.int32)
    pl.semaphore_wait(barrier, expected)

    def onward(part, i, j):
        column_first = j == b
        row_first = (i == 0) | (i == major - 1) if part == parts - 1 else jnp.bool_(False)
        along = column_first | row_first
        across = (i == a) | jnp.logical_not(row_first)
        return (
            (i >= a) & (a > 0) & along,
            (i <= a) & (a < major - 1) & along,
            (j >= b) & (b > 0) & across,
            (j <= b) & (b < minor - 1) & across,
        )

    def send_on(slot, part, h, i, j):
        for side, wanted in enumerate(onward(part, i, j)):

            @pl.when(wanted)
            def _(side=side):
                pltpu.make_async_remote_copy(
                    src_ref=held.at[slot, h, :, spans[part]],
                    dst_ref=held.at[slot, h, :, spans[part]],
                    send_sem=send_sem.at[slot, part, side],
                    recv_sem=recv_sem.at[slot, part, h],
                    device_id={"ctx": sides[side][1]},
                    device_id_type=MESH,
                ).start()

    def send_own(part, h):
        for side, wanted in enumerate(onward(part, a, b)):

            @pl.when(wanted)
            def _(side=side):
                for kind, source in enumerate((keys, values)):
                    pltpu.make_async_remote_copy(
                        src_ref=source.at[spans[part], pl.ds(h * HEAD_SIZE, HEAD_SIZE)],
                        dst_ref=held.at[me, h, kind, spans[part]],
                        send_sem=send_sem.at[me, part, side],
                        recv_sem=recv_sem.at[me, part, h],
                        device_id={"ctx": sides[side][1]},
                        device_id_type=MESH,
                    ).start()

    def settle(slot, i, j):
        for part in range(parts):
            for side, wanted in enumerate(onward(part, i, j)):

                @pl.when(wanted)
                def _(part=part, side=side):
                    pltpu.make_async_copy(
                        held.at[slot, :, :, spans[part]],
                        held.at[slot, :, :, spans[part]],
                        send_sem.at[slot, part, side],
                    ).wait()

    def find_limits(slot, carry):
        for query_block in range(blocks_here):
            my_seq = order[0, me * blocks_here + query_block]
            found = [jnp.bool_(False)] * blocks_here
            names = [order[0, slot * blocks_here + kb] for kb in range(blocks_here)]
            for entry in range(slots_live):
                listed = live[my_seq, entry]
                found = [f | (listed == name) for f, name in zip(found, names)]
            for kb in range(blocks_here):
                limits[slot, query_block, kb] = jnp.where(found[kb], HUGE, -FAR)
        return carry

    def attend(slot, h, first, after=None):
        if first:
            lanes = pl.ds(pl.multiple_of(h * HEAD_SIZE, HEAD_SIZE), HEAD_SIZE)
            keys_here, values_here = own[0, :, lanes], own[1, :, lanes]
        else:
            keys_here, values_here = held[slot, h, 0], held[slot, h, 1]
        turned_values = jnp.transpose(values_here)
        turned = (mine + 1) * per_peer
        units = [
            (q if first else (turned + q) % blocks_here, q, start)
            for q in range(blocks_here)
            for start in range(0, width, CHUNK)
        ]

        def score(u):
            query_block, q, start = units[u]
            part = jnp.dot(
                keys_here,
                turned_queries[query_block, h, :, pl.ds(start, CHUNK)],
                preferred_element_type=jnp.float32,
            )
            tops = []
            for kb in range(blocks_here):
                block = part[kb * BLOCK_TOKENS : (kb + 1) * BLOCK_TOKENS]
                if first and kb == q:
                    key_at = lax.broadcasted_iota(jnp.int32, block.shape, 0)
                    row_at = lax.broadcasted_iota(jnp.int32, block.shape, 1) % BLOCK_TOKENS
                    block = jnp.where(key_at <= row_at, block, -FAR)
                scores[u % SLOTS, pl.ds(kb * BLOCK_TOKENS, BLOCK_TOKENS), :] = block
                tops.append(jnp.max(block, axis=0, keepdims=True))
            return tops

        def absorb(u, tops):
            query_block, q, start = units[u]
            lanes = pl.ds(start, CHUNK)
            new_peak = None
            for kb, top in enumerate(tops):
                top = jnp.minimum(top, limits[slot, query_block, kb])
                new_peak = top if new_peak is None else jnp.maximum(new_peak, top)
            if not first:
                old_peak = peak[query_block, h, :, lanes]
                new_peak = jnp.maximum(new_peak, old_peak)
            peak[query_block, h, :, lanes] = new_peak
            level = new_peak * scale
            added = None
            low = []
            for kb in range(blocks_here):
                floor = jnp.maximum(level, -limits[slot, query_block, kb])
                for at in range(kb * BLOCK_TOKENS, (kb + 1) * BLOCK_TOKENS, STRIP):
                    w = jnp.exp2(scores[u % SLOTS, pl.ds(at, STRIP), :] * scale - floor)
                    added = w if added is None else added + w
                    low.append(w.astype(jnp.bfloat16))
            added = jnp.sum(added, axis=0, keepdims=True)
            product = jnp.dot(
                turned_values,
                jnp.concatenate(low, axis=0),
                preferred_element_type=jnp.float32,
            )
            if first:
                weight_sum[query_block, h, :, lanes] = added
                total[query_block, h, :, lanes] = product
            else:
                fade = jnp.exp2((old_peak - new_peak) * scale)
                weight_sum[query_block, h, :, lanes] = (
                    weight_sum[query_block, h, :, lanes] * fade + added
                )
                total[query_block, h, :, lanes] = total[query_block, h, :, lanes] * fade + product

        waiting = [score(u) for u in range(SLOTS - 1)]
        for u in range(len(units)):
            if u + SLOTS - 1 < len(units):
                waiting.append(score(u + SLOTS - 1))
            absorb(u, waiting[u])
            if after is not None and (u + 1) % (len(units) // blocks_here) == 0:
                after(units[u][1])

    per_peer = blocks_here // tp_size
    wide = kv_local * width

    def swap(turn, k, h):
        peer = (mine + turn) % tp_size
        source = pl.ds(pl.multiple_of(h * width, HEAD_SIZE), width)
        target = pl.ds(pl.multiple_of(mine * wide + h * width, HEAD_SIZE), width)
        return pltpu.make_async_remote_copy(
            src_ref=leaving.at[peer * per_peer + k, :, source],
            dst_ref=attended.at[pl.ds(k * BLOCK_TOKENS, BLOCK_TOKENS), target],
            send_sem=swap_send.at[turn - 1, k, h],
            recv_sem=swap_recv.at[turn - 1, k, h],
            device_id={"tp": peer},
            device_id_type=MESH,
        )

    def finish(h, q):
        turn, k = 1 + q // per_peer, q % per_peer
        peer = (mine + turn) % tp_size
        query_block = peer * per_peer + k
        at = pl.ds(pl.multiple_of(query_block * BLOCK_TOKENS, BLOCK_TOKENS), BLOCK_TOKENS)
        norms = []
        for g in range(groups):
            head = h * groups + g
            lanes = pl.ds(g * BLOCK_TOKENS, BLOCK_TOKENS)
            bottom = weight_sum[query_block, h, :, lanes]
            normed = total[query_block, h, :, lanes] * (1.0 / bottom)
            tile = jnp.transpose(normed.astype(jnp.bfloat16))
            if turn < tp_size:
                to = pl.multiple_of(head * HEAD_SIZE, HEAD_SIZE)
                leaving[query_block, :, pl.ds(to, HEAD_SIZE)] = tile
            else:
                to = pl.multiple_of(mine * wide + head * HEAD_SIZE, HEAD_SIZE)
                attended[pl.ds(k * BLOCK_TOKENS, BLOCK_TOKENS), pl.ds(to, HEAD_SIZE)] = tile
            norms.append(peak[query_block, h, :, lanes] * factor + jnp.log(bottom))
        heads = pl.ds(pl.multiple_of(h * groups, groups), groups)
        log_norm[heads, at] = jnp.concatenate(norms, axis=0)
        if turn < tp_size:
            swap(turn, k, h).start()

    for h in range(kv_local):
        for part in range(parts):
            send_own(part, h)
    for load in tables + loads:
        load.wait()

    def turn_block(query_block, carry):
        at = pl.ds(pl.multiple_of(query_block * BLOCK_TOKENS, BLOCK_TOKENS), BLOCK_TOKENS)
        for h in range(kv_local):
            for g in range(groups):
                head = h * groups + g
                turned_queries[query_block, h, :, pl.ds(g * BLOCK_TOKENS, BLOCK_TOKENS)] = (
                    jnp.transpose(raw_queries[at, pl.ds(head * HEAD_SIZE, HEAD_SIZE)])
                )
        return carry

    lax.fori_loop(0, blocks_here, turn_block, 0)
    lax.fori_loop(me, me + 1, find_limits, 0)

    def attend_own(h, carry):
        attend(me, h, True)
        return carry

    lax.fori_loop(0, kv_local, attend_own, 0)
    lax.fori_loop(0, major * minor, find_limits, 0)

    def nearest(x, n, k):
        both = jnp.minimum(x, n - 1 - x)
        away = 1 - 2 * (2 * x > n - 1).astype(jnp.int32)
        paired = ((k + 1) // 2) * (2 * (k % 2) - 1)
        return x + away * jnp.where(k <= 2 * both, paired, k - both)

    away = 1 - 2 * (2 * a > major - 1).astype(jnp.int32)
    far_i, far_j = (away > 0) * (major - 1), (2 * b <= minor - 1) * (minor - 1)
    waves = jnp.maximum(a, major - 1 - a) + jnp.maximum(b, minor - 1 - b)

    def place_of(wave, turn):
        j = nearest(b, minor, turn // 2)
        reach = wave - jnp.abs(j - b)
        i = a + reach * away * (1 - 2 * (turn % 2))
        fits = (i >= 0) & (i < major) & ((reach > 0) | ((reach == 0) & (turn % 2 == 0)))
        return fits & ((i != far_i) | (j != far_j)), i, j

    def take(slot, h, i, j, order):
        for part in order:
            pltpu.make_async_copy(
                held.at[slot, h, :, spans[part]],
                held.at[slot, h, :, spans[part]],
                recv_sem.at[slot, part, h],
            ).wait()
            send_on(slot, part, h, i, j)

    def one_turn(turn, carry):
        h = (turn // (2 * minor)) % kv_local
        fits, i, j = place_of(turn // (2 * minor * kv_local), turn % (2 * minor))

        @pl.when(fits)
        def _():
            take(i * minor + j, h, i, j, range(parts))
            attend(i * minor + j, h, False)

        return carry

    lax.fori_loop(2 * minor * kv_local, (waves + 1) * 2 * minor * kv_local, one_turn, 0)

    def settle_one(turn, carry):
        fits, i, j = place_of(turn // (2 * minor), turn % (2 * minor))

        @pl.when(fits)
        def _():
            settle(i * minor + j, i, j)

        return carry

    early = (waves - 1) * 2 * minor
    lax.fori_loop(0, early, settle_one, 0)

    def last_turn(h, carry):
        slot = far_i * minor + far_j
        take(slot, h, far_i, far_j, reversed(range(parts)))
        attend(slot, h, False, functools.partial(finish, h))
        return carry

    lax.fori_loop(0, kv_local, last_turn, 0)
    lax.fori_loop(early, (waves + 1) * 2 * minor, settle_one, 0)
    settle(far_i * minor + far_j, far_i, far_j)
    for turn in range(1, tp_size):
        for k in range(per_peer):
            for h in range(kv_local):
                swap(turn, k, h).wait()


def copy_out(attended, log_norm, attended_out, log_norm_out, sems):
    copies = [
        pltpu.make_async_copy(log_norm, log_norm_out, sems.at[0]),
        pltpu.make_async_copy(attended, attended_out, sems.at[1]),
    ]
    for copy in copies:
        copy.start()
    for copy in copies:
        copy.wait()


def body(tp_size, ctx_size, queries, rotated_key_rows, ordered_value_rows, block_order, live_blocks):
    tok_rows, own_columns = queries.shape
    kv_columns = rotated_key_rows.shape[1]
    kv_local = kv_columns // HEAD_SIZE
    heads_local = own_columns // HEAD_SIZE
    groups = heads_local // kv_local
    blocks_here = tok_rows // BLOCK_TOKENS
    width = groups * BLOCK_TOKENS
    major, minor = grid_of(ctx_size)
    cut = tok_rows // 2
    dims = (major, minor, tp_size, kv_local, groups, blocks_here, cut, live_blocks.shape[1])
    per_peer = blocks_here // tp_size
    whole = pl.BlockSpec(memory_space=pltpu.VMEM)
    apart = pl.BlockSpec(memory_space=pl.ANY)
    attended, log_norm = pl.pallas_call(
        functools.partial(kernel, dims),
        out_shape=(
            pltpu.VMEM((tok_rows // tp_size, own_columns * tp_size), jnp.bfloat16),
            pltpu.VMEM((heads_local, tok_rows), jnp.float32),
        ),
        in_specs=[apart] * 5,
        out_specs=(whole, whole),
        scratch_shapes=[
            pltpu.VMEM((ctx_size, kv_local, 2, tok_rows, HEAD_SIZE), jnp.bfloat16),
            pltpu.VMEM((2, tok_rows, kv_columns), jnp.bfloat16),
            pltpu.SMEM((1, block_order.shape[0]), jnp.int32),
            pltpu.SMEM(live_blocks.shape, jnp.int32),
            pltpu.VMEM((tok_rows, own_columns), jnp.bfloat16),
            pltpu.VMEM((blocks_here, kv_local, HEAD_SIZE, width), jnp.bfloat16),
            pltpu.VMEM((blocks_here, kv_local, HEAD_SIZE, width), jnp.float32),
            pltpu.VMEM((blocks_here, kv_local, 1, width), jnp.float32),
            pltpu.VMEM((blocks_here, kv_local, 1, width), jnp.float32),
            pltpu.VMEM((blocks_here, BLOCK_TOKENS, own_columns), jnp.bfloat16),
            pltpu.SMEM((ctx_size, blocks_here, blocks_here), jnp.float32),
            pltpu.VMEM((SLOTS, tok_rows, CHUNK), jnp.float32),
            pltpu.SemaphoreType.DMA((5,)),
            pltpu.SemaphoreType.DMA((ctx_size, 2, 4)),
            pltpu.SemaphoreType.DMA((ctx_size, 2, kv_local)),
            pltpu.SemaphoreType.DMA((tp_size - 1, per_peer, kv_local)),
            pltpu.SemaphoreType.DMA((tp_size - 1, per_peer, kv_local)),
        ],
        compiler_params=pltpu.CompilerParams(collective_id=0, has_side_effects=True),
        name="gather_attend",
    )(queries, rotated_key_rows, ordered_value_rows, block_order.reshape(1, -1), live_blocks)
    return pl.pallas_call(
        copy_out,
        out_shape=(
            jax.ShapeDtypeStruct(attended.shape, attended.dtype),
            jax.ShapeDtypeStruct(log_norm.shape, log_norm.dtype),
        ),
        in_specs=[whole, whole],
        out_specs=(apart, apart),
        scratch_shapes=[pltpu.SemaphoreType.DMA((2,))],
        name="copy_out",
    )(
        pltpu.with_memory_space_constraint(attended, pltpu.VMEM),
        pltpu.with_memory_space_constraint(log_norm, pltpu.VMEM),
    )


def solution(mesh):
    placed = (
        P(("rep", "ctx"), "tp"),
        P(("rep", "ctx"), "tp"),
        P(("rep", "ctx"), "tp"),
        P("rep"),
        P("rep", None),
    )
    return jax.shard_map(
        functools.partial(body, mesh.shape["tp"], mesh.shape["ctx"]),
        mesh=mesh,
        in_specs=placed,
        out_specs=(P(("rep", "ctx", "tp"), None), P(("rep", "tp"), "ctx")),
        check_vma=False,
    )
```

```python
import functools
import math

import jax
import jax.numpy as jnp
from jax import lax
from jax.experimental import pallas as pl
from jax.experimental.pallas import tpu as pltpu
from jax.sharding import PartitionSpec as P

HEAD_SIZE = 128
BLOCK_TOKENS = 128
CHUNK = 256
STRIP = 16
SLOTS = 4
FAR = 1e30
HUGE = 3e38
MESH = pl.DeviceIdType.MESH


def grid_of(count):
    minor = max(d for d in range(1, math.isqrt(count) + 1) if count % d == 0)
    return count // minor, minor


def kernel(
    dims,
    queries,
    keys,
    values,
    block_order,
    live_blocks,
    attended,
    log_norm,
    held,
    order,
    live,
    raw_queries,
    turned_queries,
    total,
    peak,
    weight_sum,
    leaving,
    limits,
    scores,
    load_sem,
    send_sem,
    recv_sem,
    swap_send,
    swap_recv,
):
    major, minor, tp_size, kv_local, groups, blocks_here, cut, slots_live = dims
    factor = HEAD_SIZE ** (-0.5)
    scale = factor * math.log2(math.e)
    width = groups * BLOCK_TOKENS
    rows = blocks_here * BLOCK_TOKENS
    spans = [pl.ds(0, cut), pl.ds(cut, rows - cut)]
    parts = len(spans)
    me = lax.axis_index("ctx")
    mine = lax.axis_index("tp")
    a, b = me // minor, me % minor

    tables = [
        pltpu.make_async_copy(block_order, order, load_sem.at[0, 0, 0]),
        pltpu.make_async_copy(live_blocks, live, load_sem.at[1, 0, 0]),
    ]
    loads = [
        pltpu.make_async_copy(
            source.at[:, pl.ds(h * HEAD_SIZE, HEAD_SIZE)], held.at[me, h, kind], load_sem.at[3, h, kind]
        )
        for h in range(kv_local)
        for kind, source in enumerate((keys, values))
    ]
    load_queries = pltpu.make_async_copy(queries, raw_queries, load_sem.at[2, 0, 0])
    barrier = pltpu.get_barrier_semaphore()
    sides = (
        (a > 0, me - minor),
        (a < major - 1, me + minor),
        (b > 0, me - 1),
        (b < minor - 1, me + 1),
    )
    for there, who in sides:

        @pl.when(there)
        def _(who=who):
            pl.semaphore_signal(barrier, inc=1, device_id={"ctx": who}, device_id_type=MESH)

    for turn in range(1, tp_size):
        peer = (mine + turn) % tp_size
        pl.semaphore_signal(barrier, inc=1, device_id={"tp": peer}, device_id_type=MESH)
    for load in loads + [load_queries] + tables:
        load.start()
    expected = jnp.int32(tp_size - 1)
    for there, _ in sides:
        expected = expected + there.astype(jnp.int32)
    pl.semaphore_wait(barrier, expected)

    def onward(part, i, j):
        column_first = j == b
        row_first = (i == 0) | (i == major - 1) if part == parts - 1 else jnp.bool_(False)
        along = column_first | row_first
        across = (i == a) | jnp.logical_not(row_first)
        return (
            (i >= a) & (a > 0) & along,
            (i <= a) & (a < major - 1) & along,
            (j >= b) & (b > 0) & across,
            (j <= b) & (b < minor - 1) & across,
        )

    def send_on(slot, part, h, i, j):
        for side, wanted in enumerate(onward(part, i, j)):

            @pl.when(wanted)
            def _(side=side):
                pltpu.make_async_remote_copy(
                    src_ref=held.at[slot, h, :, spans[part]],
                    dst_ref=held.at[slot, h, :, spans[part]],
                    send_sem=send_sem.at[slot, part, side],
                    recv_sem=recv_sem.at[slot, part, h],
                    device_id={"ctx": sides[side][1]},
                    device_id_type=MESH,
                ).start()

    def settle(slot, i, j):
        for part in range(parts):
            for side, wanted in enumerate(onward(part, i, j)):

                @pl.when(wanted)
                def _(part=part, side=side):
                    pltpu.make_async_copy(
                        held.at[slot, :, :, spans[part]],
                        held.at[slot, :, :, spans[part]],
                        send_sem.at[slot, part, side],
                    ).wait()

    def find_limits(slot, carry):
        for query_block in range(blocks_here):
            my_seq = order[0, me * blocks_here + query_block]
            found = [jnp.bool_(False)] * blocks_here
            names = [order[0, slot * blocks_here + kb] for kb in range(blocks_here)]
            for entry in range(slots_live):
                listed = live[my_seq, entry]
                found = [f | (listed == name) for f, name in zip(found, names)]
            for kb in range(blocks_here):
                limits[slot, query_block, kb] = jnp.where(found[kb], HUGE, -FAR)
        return carry

    def attend(slots, h, first, after=None):
        keys_here = [held[slot, h, 0] for slot in slots]
        turned_values = jnp.concatenate([jnp.transpose(held[slot, h, 1]) for slot in slots], axis=1)
        turned = (mine + 1) * per_peer
        units = [
            (q if first else (turned + q) % blocks_here, q, start)
            for q in range(blocks_here)
            for start in range(0, width, CHUNK)
        ]
        blocks = [(n, slot, kb) for n, slot in enumerate(slots) for kb in range(blocks_here)]

        def score(u):
            query_block, q, start = units[u]
            turned_here = turned_queries[query_block, h, :, pl.ds(start, CHUNK)]
            parts = [
                jnp.dot(k, turned_here, preferred_element_type=jnp.float32) for k in keys_here
            ]
            tops = []
            for n, slot, kb in blocks:
                block = parts[n][kb * BLOCK_TOKENS : (kb + 1) * BLOCK_TOKENS]
                if first and kb == q:
                    key_at = lax.broadcasted_iota(jnp.int32, block.shape, 0)
                    row_at = lax.broadcasted_iota(jnp.int32, block.shape, 1) % BLOCK_TOKENS
                    block = jnp.where(key_at <= row_at, block, -FAR)
                at = n * rows + kb * BLOCK_TOKENS
                scores[u % SLOTS, pl.ds(at, BLOCK_TOKENS), :] = block
                tops.append(jnp.max(block, axis=0, keepdims=True))
            return tops

        def absorb(u, tops):
            query_block, q, start = units[u]
            lanes = pl.ds(start, CHUNK)
            new_peak = None
            for (n, slot, kb), top in zip(blocks, tops):
                top = jnp.minimum(top, limits[slot, query_block, kb])
                new_peak = top if new_peak is None else jnp.maximum(new_peak, top)
            if not first:
                old_peak = peak[query_block, h, :, lanes]
                new_peak = jnp.maximum(new_peak, old_peak)
            peak[query_block, h, :, lanes] = new_peak
            level = new_peak * scale
            added = None
            low = []
            for n, slot, kb in blocks:
                floor = jnp.maximum(level, -limits[slot, query_block, kb])
                start_at = n * rows + kb * BLOCK_TOKENS
                for at in range(start_at, start_at + BLOCK_TOKENS, STRIP):
                    w = jnp.exp2(scores[u % SLOTS, pl.ds(at, STRIP), :] * scale - floor)
                    added = w if added is None else added + w
                    low.append(w.astype(jnp.bfloat16))
            added = jnp.sum(added, axis=0, keepdims=True)
            product = jnp.dot(
                turned_values,
                jnp.concatenate(low, axis=0),
                preferred_element_type=jnp.float32,
            )
            if first:
                weight_sum[query_block, h, :, lanes] = added
                total[query_block, h, :, lanes] = product
            else:
                fade = jnp.exp2((old_peak - new_peak) * scale)
                weight_sum[query_block, h, :, lanes] = (
                    weight_sum[query_block, h, :, lanes] * fade + added
                )
                total[query_block, h, :, lanes] = total[query_block, h, :, lanes] * fade + product

        waiting = [score(u) for u in range(SLOTS - 1)]
        for u in range(len(units)):
            if u + SLOTS - 1 < len(units):
                waiting.append(score(u + SLOTS - 1))
            absorb(u, waiting[u])
            if after is not None and (u + 1) % (len(units) // blocks_here) == 0:
                after(units[u][1])

    per_peer = blocks_here // tp_size
    wide = kv_local * width

    def swap(turn, k, h):
        peer = (mine + turn) % tp_size
        source = pl.ds(pl.multiple_of(h * width, HEAD_SIZE), width)
        target = pl.ds(pl.multiple_of(mine * wide + h * width, HEAD_SIZE), width)
        return pltpu.make_async_remote_copy(
            src_ref=leaving.at[peer * per_peer + k, :, source],
            dst_ref=attended.at[pl.ds(k * BLOCK_TOKENS, BLOCK_TOKENS), target],
            send_sem=swap_send.at[turn - 1, k, h],
            recv_sem=swap_recv.at[turn - 1, k, h],
            device_id={"tp": peer},
            device_id_type=MESH,
        )

    def finish(h, q):
        turn, k = 1 + q // per_peer, q % per_peer
        peer = (mine + turn) % tp_size
        query_block = peer * per_peer + k
        at = pl.ds(pl.multiple_of(query_block * BLOCK_TOKENS, BLOCK_TOKENS), BLOCK_TOKENS)
        norms = []
        for g in range(groups):
            head = h * groups + g
            lanes = pl.ds(g * BLOCK_TOKENS, BLOCK_TOKENS)
            bottom = weight_sum[query_block, h, :, lanes]
            normed = total[query_block, h, :, lanes] * (1.0 / bottom)
            tile = jnp.transpose(normed.astype(jnp.bfloat16))
            if turn < tp_size:
                to = pl.multiple_of(head * HEAD_SIZE, HEAD_SIZE)
                leaving[query_block, :, pl.ds(to, HEAD_SIZE)] = tile
            else:
                to = pl.multiple_of(mine * wide + head * HEAD_SIZE, HEAD_SIZE)
                attended[pl.ds(k * BLOCK_TOKENS, BLOCK_TOKENS), pl.ds(to, HEAD_SIZE)] = tile
            norms.append(peak[query_block, h, :, lanes] * factor + jnp.log(bottom))
        heads = pl.ds(pl.multiple_of(h * groups, groups), groups)
        log_norm[heads, at] = jnp.concatenate(norms, axis=0)
        if turn < tp_size:
            swap(turn, k, h).start()

    for load in loads:
        load.wait()
    for h in range(kv_local):
        for part in range(parts):
            send_on(me, part, h, a, b)
    for load in [load_queries] + tables:
        load.wait()

    def turn_block(query_block, carry):
        at = pl.ds(pl.multiple_of(query_block * BLOCK_TOKENS, BLOCK_TOKENS), BLOCK_TOKENS)
        for h in range(kv_local):
            for g in range(groups):
                head = h * groups + g
                turned_queries[query_block, h, :, pl.ds(g * BLOCK_TOKENS, BLOCK_TOKENS)] = (
                    jnp.transpose(raw_queries[at, pl.ds(head * HEAD_SIZE, HEAD_SIZE)])
                )
        return carry

    lax.fori_loop(0, blocks_here, turn_block, 0)
    lax.fori_loop(me, me + 1, find_limits, 0)

    def attend_own(h, carry):
        attend([me], h, True)
        return carry

    lax.fori_loop(0, kv_local, attend_own, 0)
    lax.fori_loop(0, major * minor, find_limits, 0)

    def nearest(x, n, k):
        both = jnp.minimum(x, n - 1 - x)
        away = 1 - 2 * (2 * x > n - 1).astype(jnp.int32)
        paired = ((k + 1) // 2) * (2 * (k % 2) - 1)
        return x + away * jnp.where(k <= 2 * both, paired, k - both)

    inner = (a > 0) & (a < major - 1)
    lag = 1 + inner.astype(jnp.int32)
    both = 2 * (major - 1 - lag)

    def place_of(n):
        later = n - lag
        column = (n < lag) | ((later < both) & (later % 2 == 1))
        k = jnp.where(later < both, later // 2, later - both // 2)
        k = jnp.where(n < lag, n + 1, k + column * (lag + 1))
        l = jnp.where(column, 0, 1)
        if minor > 2:
            rest = n - (2 * major - 1)
            k = jnp.where(rest >= 0, rest % major, k)
            l = jnp.where(rest >= 0, rest // major + 2, l)
        i, j = nearest(a, major, k), nearest(b, minor, l)
        return i * minor + j, i, j

    def take_part(slot, part, h, i, j):
        pltpu.make_async_copy(
            held.at[slot, h, :, spans[part]],
            held.at[slot, h, :, spans[part]],
            recv_sem.at[slot, part, h],
        ).wait()
        send_on(slot, part, h, i, j)

    ahead = minor == 2 and major == 4

    def take(place, h):
        slot, i, j = place
        for part in range(parts - 1):
            take_part(slot, part, h, i, j)
        passed = inner & (j != b) & ((i == 0) | (i == major - 1)) if ahead else jnp.bool_(False)

        @pl.when(jnp.logical_not(passed))
        def _():
            take_part(slot, parts - 1, h, i, j)

    shards = major * minor
    pairs = (shards - 2) // 2
    far = place_of(jnp.int32(shards - 2))

    def one_pair(turn, carry):
        pair, h = turn // kv_local, turn % kv_local
        here = [place_of(2 * pair + n) for n in range(2)]
        for place in here:
            take(place, h)
        if ahead:

            @pl.when(inner & (pair >= pairs - 2))
            def _():
                _, far_i, far_j = far
                i = jnp.where(pair == pairs - 1, far_i, major - 1 - far_i)
                take_part(i * minor + far_j, parts - 1, h, i, far_j)

        attend([place[0] for place in here], h, False)
        return carry

    lax.fori_loop(0, pairs * kv_local, one_pair, 0)

    def last_turn(h, carry):
        take(far, h)
        attend([far[0]], h, False, functools.partial(finish, h))
        return carry

    lax.fori_loop(0, kv_local, last_turn, 0)
    settle(me, a, b)

    def settle_one(n, carry):
        settle(*place_of(n))
        return carry

    lax.fori_loop(0, shards - 1, settle_one, 0)
    for turn in range(1, tp_size):
        for k in range(per_peer):
            for h in range(kv_local):
                swap(turn, k, h).wait()


def copy_out(attended, log_norm, attended_out, log_norm_out, sems):
    copies = [
        pltpu.make_async_copy(log_norm, log_norm_out, sems.at[0]),
        pltpu.make_async_copy(attended, attended_out, sems.at[1]),
    ]
    for copy in copies:
        copy.start()
    for copy in copies:
        copy.wait()


def body(tp_size, ctx_size, queries, rotated_key_rows, ordered_value_rows, block_order, live_blocks):
    tok_rows, own_columns = queries.shape
    kv_columns = rotated_key_rows.shape[1]
    kv_local = kv_columns // HEAD_SIZE
    heads_local = own_columns // HEAD_SIZE
    groups = heads_local // kv_local
    blocks_here = tok_rows // BLOCK_TOKENS
    width = groups * BLOCK_TOKENS
    major, minor = grid_of(ctx_size)
    cut = tok_rows // 2
    dims = (major, minor, tp_size, kv_local, groups, blocks_here, cut, live_blocks.shape[1])
    per_peer = blocks_here // tp_size
    whole = pl.BlockSpec(memory_space=pltpu.VMEM)
    apart = pl.BlockSpec(memory_space=pl.ANY)
    attended, log_norm = pl.pallas_call(
        functools.partial(kernel, dims),
        out_shape=(
            pltpu.VMEM((tok_rows // tp_size, own_columns * tp_size), jnp.bfloat16),
            pltpu.VMEM((heads_local, tok_rows), jnp.float32),
        ),
        in_specs=[apart] * 5,
        out_specs=(whole, whole),
        scratch_shapes=[
            pltpu.VMEM((ctx_size, kv_local, 2, tok_rows, HEAD_SIZE), jnp.bfloat16),
            pltpu.SMEM((1, block_order.shape[0]), jnp.int32),
            pltpu.SMEM(live_blocks.shape, jnp.int32),
            pltpu.VMEM((tok_rows, own_columns), jnp.bfloat16),
            pltpu.VMEM((blocks_here, kv_local, HEAD_SIZE, width), jnp.bfloat16),
            pltpu.VMEM((blocks_here, kv_local, HEAD_SIZE, width), jnp.float32),
            pltpu.VMEM((blocks_here, kv_local, 1, width), jnp.float32),
            pltpu.VMEM((blocks_here, kv_local, 1, width), jnp.float32),
            pltpu.VMEM((blocks_here, BLOCK_TOKENS, own_columns), jnp.bfloat16),
            pltpu.SMEM((ctx_size, blocks_here, blocks_here), jnp.float32),
            pltpu.VMEM((SLOTS, 2 * tok_rows, CHUNK), jnp.float32),
            pltpu.SemaphoreType.DMA((4, kv_local, 2)),
            pltpu.SemaphoreType.DMA((ctx_size, 2, 4)),
            pltpu.SemaphoreType.DMA((ctx_size, 2, kv_local)),
            pltpu.SemaphoreType.DMA((tp_size - 1, per_peer, kv_local)),
            pltpu.SemaphoreType.DMA((tp_size - 1, per_peer, kv_local)),
        ],
        compiler_params=pltpu.CompilerParams(collective_id=0, has_side_effects=True),
        name="gather_attend",
    )(queries, rotated_key_rows, ordered_value_rows, block_order.reshape(1, -1), live_blocks)
    return pl.pallas_call(
        copy_out,
        out_shape=(
            jax.ShapeDtypeStruct(attended.shape, attended.dtype),
            jax.ShapeDtypeStruct(log_norm.shape, log_norm.dtype),
        ),
        in_specs=[whole, whole],
        out_specs=(apart, apart),
        scratch_shapes=[pltpu.SemaphoreType.DMA((2,))],
        name="copy_out",
    )(
        pltpu.with_memory_space_constraint(attended, pltpu.VMEM),
        pltpu.with_memory_space_constraint(log_norm, pltpu.VMEM),
    )


def solution(mesh):
    placed = (
        P(("rep", "ctx"), "tp"),
        P(("rep", "ctx"), "tp"),
        P(("rep", "ctx"), "tp"),
        P("rep"),
        P("rep", None),
    )
    return jax.shard_map(
        functools.partial(body, mesh.shape["tp"], mesh.shape["ctx"]),
        mesh=mesh,
        in_specs=placed,
        out_specs=(P(("rep", "ctx", "tp"), None), P(("rep", "tp"), "ctx")),
        check_vma=False,
    )
```

```python
import functools
import math

import jax
import jax.numpy as jnp
from jax import lax
from jax.experimental import pallas as pl
from jax.experimental.pallas import tpu as pltpu
from jax.sharding import PartitionSpec as P

HEAD_SIZE = 128
BLOCK_TOKENS = 128
CHUNK = 256
STRIP = 16
SLOTS = 4
FAR = 1e30
HUGE = 3e38
MESH = pl.DeviceIdType.MESH


def grid_of(count):
    minor = max(d for d in range(1, math.isqrt(count) + 1) if count % d == 0)
    return count // minor, minor


def kernel(
    dims,
    queries,
    keys,
    values,
    block_order,
    live_blocks,
    attended,
    log_norm,
    held,
    order,
    live,
    raw_queries,
    turned_queries,
    total,
    peak,
    weight_sum,
    leaving,
    limits,
    scores,
    load_sem,
    answer,
    send_sem,
    recv_sem,
    swap_send,
    swap_recv,
):
    major, minor, tp_size, kv_local, groups, blocks_here, cut, slots_live = dims
    factor = HEAD_SIZE ** (-0.5)
    scale = factor * math.log2(math.e)
    width = groups * BLOCK_TOKENS
    rows = blocks_here * BLOCK_TOKENS
    spans = [pl.ds(0, cut), pl.ds(cut, rows - cut)]
    parts = len(spans)
    me = lax.axis_index("ctx")
    mine = lax.axis_index("tp")
    a, b = me // minor, me % minor

    tables = [
        pltpu.make_async_copy(block_order, order, load_sem.at[0, 0, 0]),
        pltpu.make_async_copy(live_blocks, live, load_sem.at[1, 0, 0]),
    ]
    loads = [
        pltpu.make_async_copy(
            source.at[:, pl.ds(h * HEAD_SIZE, HEAD_SIZE)], held.at[me, h, kind], load_sem.at[3, h, kind]
        )
        for h in range(kv_local)
        for kind, source in enumerate((keys, values))
    ]
    load_queries = pltpu.make_async_copy(queries, raw_queries, load_sem.at[2, 0, 0])
    barrier = pltpu.get_barrier_semaphore()
    sides = (
        (a > 0, me - minor),
        (a < major - 1, me + minor),
        (b > 0, me - 1),
        (b < minor - 1, me + 1),
    )
    lower, upper = (0, 2), (1, 3)
    for side in upper:
        there, who = sides[side]

        @pl.when(there)
        def _(who=who):
            pl.semaphore_signal(barrier, inc=1, device_id={"ctx": who}, device_id_type=MESH)

    for turn in range(1, tp_size):
        peer = (mine + turn) % tp_size
        pl.semaphore_signal(barrier, inc=1, device_id={"tp": peer}, device_id_type=MESH)
    for load in loads + [load_queries] + tables:
        load.start()
    expected = jnp.int32(tp_size - 1)
    for side in lower:
        expected = expected + sides[side][0].astype(jnp.int32)
    pl.semaphore_wait(barrier, expected)
    for side in lower:
        there, who = sides[side]

        @pl.when(there)
        def _(who=who, side=side):
            pl.semaphore_signal(
                answer.at[side // 2], inc=1, device_id={"ctx": who}, device_id_type=MESH
            )

    def onward(part, i, j):
        column_first = j == b
        row_first = (i == 0) | (i == major - 1) if part == parts - 1 else jnp.bool_(False)
        along = column_first | row_first
        across = (i == a) | jnp.logical_not(row_first)
        return (
            (i >= a) & (a > 0) & along,
            (i <= a) & (a < major - 1) & along,
            (j >= b) & (b > 0) & across,
            (j <= b) & (b < minor - 1) & across,
        )

    def send_on(slot, part, h, i, j, to=range(4)):
        wanted = onward(part, i, j)
        for side in to:

            @pl.when(wanted[side])
            def _(side=side):
                pltpu.make_async_remote_copy(
                    src_ref=held.at[slot, h, :, spans[part]],
                    dst_ref=held.at[slot, h, :, spans[part]],
                    send_sem=send_sem.at[slot, part, side],
                    recv_sem=recv_sem.at[slot, part, h],
                    device_id={"ctx": sides[side][1]},
                    device_id_type=MESH,
                ).start()

    def send_own(part, h, to):
        wanted = onward(part, a, b)
        for side in to:

            @pl.when(wanted[side])
            def _(side=side):
                for kind, source in enumerate((keys, values)):
                    pltpu.make_async_remote_copy(
                        src_ref=source.at[spans[part], pl.ds(h * HEAD_SIZE, HEAD_SIZE)],
                        dst_ref=held.at[me, h, kind, spans[part]],
                        send_sem=send_sem.at[me, part, side],
                        recv_sem=recv_sem.at[me, part, h],
                        device_id={"ctx": sides[side][1]},
                        device_id_type=MESH,
                    ).start()

    def settle(slot, i, j):
        for part in range(parts):
            for side, wanted in enumerate(onward(part, i, j)):

                @pl.when(wanted)
                def _(part=part, side=side):
                    pltpu.make_async_copy(
                        held.at[slot, :, :, spans[part]],
                        held.at[slot, :, :, spans[part]],
                        send_sem.at[slot, part, side],
                    ).wait()

    def find_limits(slot, carry):
        for query_block in range(blocks_here):
            my_seq = order[0, me * blocks_here + query_block]
            found = [jnp.bool_(False)] * blocks_here
            names = [order[0, slot * blocks_here + kb] for kb in range(blocks_here)]
            for entry in range(slots_live):
                listed = live[my_seq, entry]
                found = [f | (listed == name) for f, name in zip(found, names)]
            for kb in range(blocks_here):
                limits[slot, query_block, kb] = jnp.where(found[kb], HUGE, -FAR)
        return carry

    def attend(slots, h, first, after=None):
        keys_here = [held[slot, h, 0] for slot in slots]
        turned_values = jnp.concatenate([jnp.transpose(held[slot, h, 1]) for slot in slots], axis=1)
        ones = jnp.ones((16, turned_values.shape[1]), turned_values.dtype)
        turned_values = jnp.concatenate([turned_values, ones], axis=0)
        turned = (mine + 1) * per_peer
        units = [
            (q if first else (turned + q) % blocks_here, q, start)
            for q in range(blocks_here)
            for start in range(0, width, CHUNK)
        ]
        blocks = [(n, slot, kb) for n, slot in enumerate(slots) for kb in range(blocks_here)]

        def score(u):
            query_block, q, start = units[u]
            turned_here = turned_queries[query_block, h, :, pl.ds(start, CHUNK)]
            parts = [
                jnp.dot(k, turned_here, preferred_element_type=jnp.float32) for k in keys_here
            ]
            tops = []
            for n, slot, kb in blocks:
                block = parts[n][kb * BLOCK_TOKENS : (kb + 1) * BLOCK_TOKENS]
                if first and kb == q:
                    key_at = lax.broadcasted_iota(jnp.int32, block.shape, 0)
                    row_at = lax.broadcasted_iota(jnp.int32, block.shape, 1) % BLOCK_TOKENS
                    block = jnp.where(key_at <= row_at, block, -FAR)
                at = n * rows + kb * BLOCK_TOKENS
                scores[u % SLOTS, pl.ds(at, BLOCK_TOKENS), :] = block
                tops.append(jnp.max(block, axis=0, keepdims=True))
            return tops

        def absorb(u, tops):
            query_block, q, start = units[u]
            lanes = pl.ds(start, CHUNK)
            new_peak = None
            for (n, slot, kb), top in zip(blocks, tops):
                top = jnp.minimum(top, limits[slot, query_block, kb])
                new_peak = top if new_peak is None else jnp.maximum(new_peak, top)
            if not first:
                old_peak = peak[query_block, h, :, lanes]
                new_peak = jnp.maximum(new_peak, old_peak)
            peak[query_block, h, :, lanes] = new_peak
            level = new_peak * scale
            added = None
            low = []
            for n, slot, kb in blocks:
                floor = jnp.maximum(level, -limits[slot, query_block, kb])
                start_at = n * rows + kb * BLOCK_TOKENS
                for at in range(start_at, start_at + BLOCK_TOKENS, STRIP):
                    w = jnp.exp2(scores[u % SLOTS, pl.ds(at, STRIP), :] * scale - floor)
                    low.append(w.astype(jnp.bfloat16))
            product = jnp.dot(
                turned_values,
                jnp.concatenate(low, axis=0),
                preferred_element_type=jnp.float32,
            )
            added, product = product[HEAD_SIZE : HEAD_SIZE + 1], product[:HEAD_SIZE]
            if first:
                weight_sum[query_block, h, :, lanes] = added
                total[query_block, h, :, lanes] = product
            else:
                fade = jnp.exp2((old_peak - new_peak) * scale)
                weight_sum[query_block, h, :, lanes] = (
                    weight_sum[query_block, h, :, lanes] * fade + added
                )
                total[query_block, h, :, lanes] = total[query_block, h, :, lanes] * fade + product

        waiting = [score(u) for u in range(SLOTS - 1)]
        for u in range(len(units)):
            if u + SLOTS - 1 < len(units):
                waiting.append(score(u + SLOTS - 1))
            absorb(u, waiting[u])
            if after is not None and (u + 1) % (len(units) // blocks_here) == 0:
                after(units[u][1])

    per_peer = blocks_here // tp_size
    wide = kv_local * width

    def swap(turn, k, h):
        peer = (mine + turn) % tp_size
        source = pl.ds(pl.multiple_of(h * width, HEAD_SIZE), width)
        target = pl.ds(pl.multiple_of(mine * wide + h * width, HEAD_SIZE), width)
        return pltpu.make_async_remote_copy(
            src_ref=leaving.at[peer * per_peer + k, :, source],
            dst_ref=attended.at[pl.ds(k * BLOCK_TOKENS, BLOCK_TOKENS), target],
            send_sem=swap_send.at[turn - 1, k, h],
            recv_sem=swap_recv.at[turn - 1, k, h],
            device_id={"tp": peer},
            device_id_type=MESH,
        )

    def finish(h, q):
        turn, k = 1 + q // per_peer, q % per_peer
        peer = (mine + turn) % tp_size
        query_block = peer * per_peer + k
        at = pl.ds(pl.multiple_of(query_block * BLOCK_TOKENS, BLOCK_TOKENS), BLOCK_TOKENS)
        norms = []
        for g in range(groups):
            head = h * groups + g
            lanes = pl.ds(g * BLOCK_TOKENS, BLOCK_TOKENS)
            bottom = weight_sum[query_block, h, :, lanes]
            normed = total[query_block, h, :, lanes] * (1.0 / bottom)
            tile = jnp.transpose(normed.astype(jnp.bfloat16))
            if turn < tp_size:
                to = pl.multiple_of(head * HEAD_SIZE, HEAD_SIZE)
                leaving[query_block, :, pl.ds(to, HEAD_SIZE)] = tile
            else:
                to = pl.multiple_of(mine * wide + head * HEAD_SIZE, HEAD_SIZE)
                attended[pl.ds(k * BLOCK_TOKENS, BLOCK_TOKENS), pl.ds(to, HEAD_SIZE)] = tile
            norms.append(peak[query_block, h, :, lanes] * factor + jnp.log(bottom))
        heads = pl.ds(pl.multiple_of(h * groups, groups), groups)
        log_norm[heads, at] = jnp.concatenate(norms, axis=0)
        if turn < tp_size:
            swap(turn, k, h).start()

    for part in range(parts):
        send_own(part, 0, lower)
    for load in loads:
        load.wait()
    for h in range(1, kv_local):
        for part in range(parts):
            send_on(me, part, h, a, b, lower)
    for side in upper:

        @pl.when(sides[side][0])
        def _(side=side):
            pl.semaphore_wait(answer.at[side // 2], 1)

    for h in range(kv_local):
        for part in range(parts):
            send_on(me, part, h, a, b, upper)
    for load in [load_queries] + tables:
        load.wait()

    def turn_block(query_block, carry):
        at = pl.ds(pl.multiple_of(query_block * BLOCK_TOKENS, BLOCK_TOKENS), BLOCK_TOKENS)
        for h in range(kv_local):
            for g in range(groups):
                head = h * groups + g
                turned_queries[query_block, h, :, pl.ds(g * BLOCK_TOKENS, BLOCK_TOKENS)] = (
                    jnp.transpose(raw_queries[at, pl.ds(head * HEAD_SIZE, HEAD_SIZE)])
                )
        return carry

    lax.fori_loop(0, blocks_here, turn_block, 0)
    lax.fori_loop(me, me + 1, find_limits, 0)

    def attend_own(h, carry):
        attend([me], h, True)
        return carry

    lax.fori_loop(0, kv_local, attend_own, 0)
    lax.fori_loop(0, major * minor, find_limits, 0)

    def nearest(x, n, k):
        both = jnp.minimum(x, n - 1 - x)
        away = 1 - 2 * (2 * x > n - 1).astype(jnp.int32)
        paired = ((k + 1) // 2) * (2 * (k % 2) - 1)
        return x + away * jnp.where(k <= 2 * both, paired, k - both)

    inner = (a > 0) & (a < major - 1)
    lag = 1 + inner.astype(jnp.int32)
    both = 2 * (major - 1 - lag)

    def place_of(n):
        later = n - lag
        column = (n < lag) | ((later < both) & (later % 2 == 1))
        k = jnp.where(later < both, later // 2, later - both // 2)
        k = jnp.where(n < lag, n + 1, k + column * (lag + 1))
        l = jnp.where(column, 0, 1)
        if minor > 2:
            rest = n - (2 * major - 1)
            k = jnp.where(rest >= 0, rest % major, k)
            l = jnp.where(rest >= 0, rest // major + 2, l)
        i, j = nearest(a, major, k), nearest(b, minor, l)
        return i * minor + j, i, j

    def take_part(slot, part, h, i, j):
        pltpu.make_async_copy(
            held.at[slot, h, :, spans[part]],
            held.at[slot, h, :, spans[part]],
            recv_sem.at[slot, part, h],
        ).wait()
        send_on(slot, part, h, i, j)

    ahead = minor == 2 and major == 4

    def take(place, h):
        slot, i, j = place
        for part in range(parts - 1):
            take_part(slot, part, h, i, j)
        passed = inner & (j != b) & ((i == 0) | (i == major - 1)) if ahead else jnp.bool_(False)

        @pl.when(jnp.logical_not(passed))
        def _():
            take_part(slot, parts - 1, h, i, j)

    shards = major * minor
    pairs = (shards - 2) // 2
    far = place_of(jnp.int32(shards - 2))

    def one_pair(turn, carry):
        pair, h = turn // kv_local, turn % kv_local
        here = [place_of(2 * pair + n) for n in range(2)]
        for place in here:
            take(place, h)
        if ahead:

            @pl.when(inner & (pair >= pairs - 2))
            def _():
                _, far_i, far_j = far
                i = jnp.where(pair == pairs - 1, far_i, major - 1 - far_i)
                take_part(i * minor + far_j, parts - 1, h, i, far_j)

        attend([place[0] for place in here], h, False)
        return carry

    lax.fori_loop(0, pairs * kv_local, one_pair, 0)

    def last_turn(h, carry):
        take(far, h)
        attend([far[0]], h, False, functools.partial(finish, h))
        return carry

    lax.fori_loop(0, kv_local, last_turn, 0)
    settle(me, a, b)

    def settle_one(n, carry):
        settle(*place_of(n))
        return carry

    lax.fori_loop(0, shards - 1, settle_one, 0)
    for turn in range(1, tp_size):
        for k in range(per_peer):
            for h in range(kv_local):
                swap(turn, k, h).wait()


def copy_out(attended, log_norm, attended_out, log_norm_out, sems):
    copies = [
        pltpu.make_async_copy(log_norm, log_norm_out, sems.at[0]),
        pltpu.make_async_copy(attended, attended_out, sems.at[1]),
    ]
    for copy in copies:
        copy.start()
    for copy in copies:
        copy.wait()


def body(tp_size, ctx_size, queries, rotated_key_rows, ordered_value_rows, block_order, live_blocks):
    tok_rows, own_columns = queries.shape
    kv_columns = rotated_key_rows.shape[1]
    kv_local = kv_columns // HEAD_SIZE
    heads_local = own_columns // HEAD_SIZE
    groups = heads_local // kv_local
    blocks_here = tok_rows // BLOCK_TOKENS
    width = groups * BLOCK_TOKENS
    major, minor = grid_of(ctx_size)
    cut = tok_rows // 2
    dims = (major, minor, tp_size, kv_local, groups, blocks_here, cut, live_blocks.shape[1])
    per_peer = blocks_here // tp_size
    whole = pl.BlockSpec(memory_space=pltpu.VMEM)
    apart = pl.BlockSpec(memory_space=pl.ANY)
    attended, log_norm = pl.pallas_call(
        functools.partial(kernel, dims),
        out_shape=(
            pltpu.VMEM((tok_rows // tp_size, own_columns * tp_size), jnp.bfloat16),
            pltpu.VMEM((heads_local, tok_rows), jnp.float32),
        ),
        in_specs=[apart] * 5,
        out_specs=(whole, whole),
        scratch_shapes=[
            pltpu.VMEM((ctx_size, kv_local, 2, tok_rows, HEAD_SIZE), jnp.bfloat16),
            pltpu.SMEM((1, block_order.shape[0]), jnp.int32),
            pltpu.SMEM(live_blocks.shape, jnp.int32),
            pltpu.VMEM((tok_rows, own_columns), jnp.bfloat16),
            pltpu.VMEM((blocks_here, kv_local, HEAD_SIZE, width), jnp.bfloat16),
            pltpu.VMEM((blocks_here, kv_local, HEAD_SIZE, width), jnp.float32),
            pltpu.VMEM((blocks_here, kv_local, 1, width), jnp.float32),
            pltpu.VMEM((blocks_here, kv_local, 1, width), jnp.float32),
            pltpu.VMEM((blocks_here, BLOCK_TOKENS, own_columns), jnp.bfloat16),
            pltpu.SMEM((ctx_size, blocks_here, blocks_here), jnp.float32),
            pltpu.VMEM((SLOTS, 2 * tok_rows, CHUNK), jnp.float32),
            pltpu.SemaphoreType.DMA((4, kv_local, 2)),
            pltpu.SemaphoreType.REGULAR((2,)),
            pltpu.SemaphoreType.DMA((ctx_size, 2, 4)),
            pltpu.SemaphoreType.DMA((ctx_size, 2, kv_local)),
            pltpu.SemaphoreType.DMA((tp_size - 1, per_peer, kv_local)),
            pltpu.SemaphoreType.DMA((tp_size - 1, per_peer, kv_local)),
        ],
        compiler_params=pltpu.CompilerParams(collective_id=0, has_side_effects=True),
        name="gather_attend",
    )(queries, rotated_key_rows, ordered_value_rows, block_order.reshape(1, -1), live_blocks)
    return pl.pallas_call(
        copy_out,
        out_shape=(
            jax.ShapeDtypeStruct(attended.shape, attended.dtype),
            jax.ShapeDtypeStruct(log_norm.shape, log_norm.dtype),
        ),
        in_specs=[whole, whole],
        out_specs=(apart, apart),
        scratch_shapes=[pltpu.SemaphoreType.DMA((2,))],
        name="copy_out",
    )(
        pltpu.with_memory_space_constraint(attended, pltpu.VMEM),
        pltpu.with_memory_space_constraint(log_norm, pltpu.VMEM),
    )


def solution(mesh):
    placed = (
        P(("rep", "ctx"), "tp"),
        P(("rep", "ctx"), "tp"),
        P(("rep", "ctx"), "tp"),
        P("rep"),
        P("rep", None),
    )
    return jax.shard_map(
        functools.partial(body, mesh.shape["tp"], mesh.shape["ctx"]),
        mesh=mesh,
        in_specs=placed,
        out_specs=(P(("rep", "ctx", "tp"), None), P(("rep", "tp"), "ctx")),
        check_vma=False,
    )
```

```python
import functools
import math

import jax
import jax.numpy as jnp
from jax import lax
from jax.experimental import pallas as pl
from jax.experimental.pallas import tpu as pltpu
from jax.sharding import PartitionSpec as P

HEAD_SIZE = 128
BLOCK_TOKENS = 128
CHUNK = 256
STRIP = 16
SLOTS = 4
VMEM_LIMIT = 60 << 20
FAR = 1e30
HUGE = 3e38
MESH = pl.DeviceIdType.MESH


def grid_of(count):
    minor = max(d for d in range(1, math.isqrt(count) + 1) if count % d == 0)
    return count // minor, minor


def kernel(
    dims,
    queries,
    keys,
    values,
    block_order,
    live_blocks,
    attended,
    log_norm,
    held,
    order,
    live,
    raw_queries,
    turned_queries,
    total,
    peak,
    weight_sum,
    leaving,
    limits,
    scores,
    load_sem,
    answer,
    send_sem,
    recv_sem,
    swap_send,
    swap_recv,
):
    major, minor, tp_size, kv_local, groups, blocks_here, cut, slots_live = dims
    factor = HEAD_SIZE ** (-0.5)
    scale = factor * math.log2(math.e)
    width = groups * BLOCK_TOKENS
    rows = blocks_here * BLOCK_TOKENS
    spans = [pl.ds(0, cut), pl.ds(cut, rows - cut)]
    parts = len(spans)
    me = lax.axis_index("ctx")
    mine = lax.axis_index("tp")
    a, b = me // minor, me % minor
    per_peer = blocks_here // tp_size

    def real(q):
        return ((mine + 1) * per_peer + q) % blocks_here


    tables = [
        pltpu.make_async_copy(block_order, order, load_sem.at[0, 0, 0]),
        pltpu.make_async_copy(live_blocks, live, load_sem.at[1, 0, 0]),
    ]
    loads = [
        pltpu.make_async_copy(
            source.at[:, pl.ds(h * HEAD_SIZE, HEAD_SIZE)], held.at[me, h, kind], load_sem.at[3, h, kind]
        )
        for h in range(kv_local)
        for kind, source in enumerate((keys, values))
    ]
    load_queries = pltpu.make_async_copy(queries, raw_queries, load_sem.at[2, 0, 0])
    barrier = pltpu.get_barrier_semaphore()
    sides = (
        (a > 0, me - minor),
        (a < major - 1, me + minor),
        (b > 0, me - 1),
        (b < minor - 1, me + 1),
    )
    lower, upper = (0, 2), (1, 3)
    for side in upper:
        there, who = sides[side]

        @pl.when(there)
        def _(who=who):
            pl.semaphore_signal(barrier, inc=1, device_id={"ctx": who}, device_id_type=MESH)

    for turn in range(1, tp_size):
        peer = (mine + turn) % tp_size
        pl.semaphore_signal(barrier, inc=1, device_id={"tp": peer}, device_id_type=MESH)
    for load in loads:
        load.start()
    expected = jnp.int32(tp_size - 1)
    for side in lower:
        expected = expected + sides[side][0].astype(jnp.int32)
    pl.semaphore_wait(barrier, expected)
    for side in lower:
        there, who = sides[side]

        @pl.when(there)
        def _(who=who, side=side):
            pl.semaphore_signal(
                answer.at[side // 2], inc=1, device_id={"ctx": who}, device_id_type=MESH
            )

    def onward(part, i, j):
        column_first = j == b
        row_first = (i == 0) | (i == major - 1) if part == parts - 1 else jnp.bool_(False)
        along = column_first | row_first
        across = (i == a) | jnp.logical_not(row_first)
        return (
            (i >= a) & (a > 0) & along,
            (i <= a) & (a < major - 1) & along,
            (j >= b) & (b > 0) & across,
            (j <= b) & (b < minor - 1) & across,
        )

    def send_on(slot, part, h, i, j, to=range(4)):
        wanted = onward(part, i, j)
        for side in to:

            @pl.when(wanted[side])
            def _(side=side):
                pltpu.make_async_remote_copy(
                    src_ref=held.at[slot, h, :, spans[part]],
                    dst_ref=held.at[slot, h, :, spans[part]],
                    send_sem=send_sem.at[slot, part, side],
                    recv_sem=recv_sem.at[slot, part, h],
                    device_id={"ctx": sides[side][1]},
                    device_id_type=MESH,
                ).start()

    def send_own(part, h, to):
        wanted = onward(part, a, b)
        for side in to:

            @pl.when(wanted[side])
            def _(side=side):
                for kind, source in enumerate((keys, values)):
                    pltpu.make_async_remote_copy(
                        src_ref=source.at[spans[part], pl.ds(h * HEAD_SIZE, HEAD_SIZE)],
                        dst_ref=held.at[me, h, kind, spans[part]],
                        send_sem=send_sem.at[me, part, side],
                        recv_sem=recv_sem.at[me, part, h],
                        device_id={"ctx": sides[side][1]},
                        device_id_type=MESH,
                    ).start()

    def settle(slot, i, j):
        for part in range(parts):
            for side, wanted in enumerate(onward(part, i, j)):

                @pl.when(wanted)
                def _(part=part, side=side):
                    pltpu.make_async_copy(
                        held.at[slot, :, :, spans[part]],
                        held.at[slot, :, :, spans[part]],
                        send_sem.at[slot, part, side],
                    ).wait()

    def find_limits(slot, carry):
        for q in range(blocks_here):
            my_seq = order[0, me * blocks_here + real(q)]
            found = [jnp.bool_(False)] * blocks_here
            names = [order[0, slot * blocks_here + kb] for kb in range(blocks_here)]
            for entry in range(slots_live):
                listed = live[my_seq, entry]
                found = [f | (listed == name) for f, name in zip(found, names)]
            for kb in range(blocks_here):
                limits[slot, q, kb] = jnp.where(found[kb], HUGE, -FAR)
        return carry

    def attend(slots, h, first, after=None):
        keys_here = [held[slot, h, 0] for slot in slots]
        turned_values = jnp.concatenate([jnp.transpose(held[slot, h, 1]) for slot in slots], axis=1)
        ones = jnp.ones((16, turned_values.shape[1]), turned_values.dtype)
        turned_values = jnp.concatenate([turned_values, ones], axis=0)
        units = [(q, start) for q in range(blocks_here) for start in range(0, width, CHUNK)]
        blocks = [(n, slot, kb) for n, slot in enumerate(slots) for kb in range(blocks_here)]

        def score(u):
            q, start = units[u]
            turned_here = turned_queries[q, h, :, pl.ds(start, CHUNK)]
            parts = [
                jnp.dot(k, turned_here, preferred_element_type=jnp.float32) for k in keys_here
            ]
            tops = []
            for n, slot, kb in blocks:
                block = parts[n][kb * BLOCK_TOKENS : (kb + 1) * BLOCK_TOKENS]
                if first:
                    key_at = lax.broadcasted_iota(jnp.int32, block.shape, 0)
                    row_at = lax.broadcasted_iota(jnp.int32, block.shape, 1) % BLOCK_TOKENS
                    row_at = row_at + (real(q) != kb).astype(jnp.int32) * BLOCK_TOKENS
                    block = jnp.where(key_at <= row_at, block, -FAR)
                at = n * rows + kb * BLOCK_TOKENS
                scores[u % SLOTS, pl.ds(at, BLOCK_TOKENS), :] = block
                tops.append(jnp.max(block, axis=0, keepdims=True))
            return tops

        def absorb(u, tops):
            q, start = units[u]
            lanes = pl.ds(start, CHUNK)
            new_peak = None
            for (n, slot, kb), top in zip(blocks, tops):
                top = jnp.minimum(top, limits[slot, q, kb])
                new_peak = top if new_peak is None else jnp.maximum(new_peak, top)
            if not first:
                old_peak = peak[q, h, :, lanes]
                new_peak = jnp.maximum(new_peak, old_peak)
            peak[q, h, :, lanes] = new_peak
            level = new_peak * scale
            added = None
            low = []
            for n, slot, kb in blocks:
                floor = jnp.maximum(level, -limits[slot, q, kb])
                start_at = n * rows + kb * BLOCK_TOKENS
                for at in range(start_at, start_at + BLOCK_TOKENS, STRIP):
                    w = jnp.exp2(scores[u % SLOTS, pl.ds(at, STRIP), :] * scale - floor)
                    low.append(w.astype(jnp.bfloat16))
            product = jnp.dot(
                turned_values,
                jnp.concatenate(low, axis=0),
                preferred_element_type=jnp.float32,
            )
            added, product = product[HEAD_SIZE : HEAD_SIZE + 1], product[:HEAD_SIZE]
            if first:
                weight_sum[q, h, :, lanes] = added
                total[q, h, :, lanes] = product
            else:
                fade = jnp.exp2((old_peak - new_peak) * scale)
                weight_sum[q, h, :, lanes] = (
                    weight_sum[q, h, :, lanes] * fade + added
                )
                total[q, h, :, lanes] = total[q, h, :, lanes] * fade + product

        waiting = [score(u) for u in range(SLOTS - 1)]
        for u in range(len(units)):
            if u + SLOTS - 1 < len(units):
                waiting.append(score(u + SLOTS - 1))
            absorb(u, waiting[u])
            if after is not None and (u + 1) % (len(units) // blocks_here) == 0:
                after(units[u][0])

    wide = kv_local * width

    def swap(turn, k, h):
        peer = (mine + turn) % tp_size
        source = pl.ds(pl.multiple_of(h * width, HEAD_SIZE), width)
        target = pl.ds(pl.multiple_of(mine * wide + h * width, HEAD_SIZE), width)
        return pltpu.make_async_remote_copy(
            src_ref=leaving.at[(turn - 1) * per_peer + k, :, source],
            dst_ref=attended.at[pl.ds(k * BLOCK_TOKENS, BLOCK_TOKENS), target],
            send_sem=swap_send.at[turn - 1, k, h],
            recv_sem=swap_recv.at[turn - 1, k, h],
            device_id={"tp": peer},
            device_id_type=MESH,
        )

    def finish(h, q):
        turn, k = 1 + q // per_peer, q % per_peer
        at = pl.ds(pl.multiple_of(real(q) * BLOCK_TOKENS, BLOCK_TOKENS), BLOCK_TOKENS)
        norms = []
        for g in range(groups):
            head = h * groups + g
            lanes = pl.ds(g * BLOCK_TOKENS, BLOCK_TOKENS)
            bottom = weight_sum[q, h, :, lanes]
            normed = total[q, h, :, lanes] * (1.0 / bottom)
            tile = jnp.transpose(normed.astype(jnp.bfloat16))
            if turn < tp_size:
                to = pl.multiple_of(head * HEAD_SIZE, HEAD_SIZE)
                leaving[q, :, pl.ds(to, HEAD_SIZE)] = tile
            else:
                to = pl.multiple_of(mine * wide + head * HEAD_SIZE, HEAD_SIZE)
                attended[pl.ds(k * BLOCK_TOKENS, BLOCK_TOKENS), pl.ds(to, HEAD_SIZE)] = tile
            norms.append(peak[q, h, :, lanes] * factor + jnp.log(bottom))
        heads = pl.ds(pl.multiple_of(h * groups, groups), groups)
        log_norm[heads, at] = jnp.concatenate(norms, axis=0)
        if turn < tp_size:
            swap(turn, k, h).start()

    for part in range(parts):
        send_own(part, 0, lower)
    for load in [load_queries] + tables:
        load.start()
    for load in loads:
        load.wait()
    for h in range(1, kv_local):
        for part in range(parts):
            send_on(me, part, h, a, b, lower)
    for side in upper:

        @pl.when(sides[side][0])
        def _(side=side):
            pl.semaphore_wait(answer.at[side // 2], 1)

    for h in range(kv_local):
        for part in range(parts):
            send_on(me, part, h, a, b, upper)
    for load in [load_queries] + tables:
        load.wait()

    def turn_block(q, carry):
        at = pl.ds(pl.multiple_of(real(q) * BLOCK_TOKENS, BLOCK_TOKENS), BLOCK_TOKENS)
        for h in range(kv_local):
            for g in range(groups):
                head = h * groups + g
                turned_queries[q, h, :, pl.ds(g * BLOCK_TOKENS, BLOCK_TOKENS)] = jnp.transpose(
                    raw_queries[at, pl.ds(head * HEAD_SIZE, HEAD_SIZE)]
                )
        return carry

    lax.fori_loop(0, blocks_here, turn_block, 0)
    lax.fori_loop(me, me + 1, find_limits, 0)

    def attend_own(h, carry):
        attend([me], h, True)
        return carry

    lax.fori_loop(0, kv_local, attend_own, 0)
    lax.fori_loop(0, major * minor, find_limits, 0)

    def nearest(x, n, k):
        both = jnp.minimum(x, n - 1 - x)
        away = 1 - 2 * (2 * x > n - 1).astype(jnp.int32)
        paired = ((k + 1) // 2) * (2 * (k % 2) - 1)
        return x + away * jnp.where(k <= 2 * both, paired, k - both)

    inner = (a > 0) & (a < major - 1)
    lag = 1 + inner.astype(jnp.int32)
    both = 2 * (major - 1 - lag)

    def place_of(n):
        later = n - lag
        column = (n < lag) | ((later < both) & (later % 2 == 1))
        k = jnp.where(later < both, later // 2, later - both // 2)
        k = jnp.where(n < lag, n + 1, k + column * (lag + 1))
        l = jnp.where(column, 0, 1)
        if minor > 2:
            rest = n - (2 * major - 1)
            k = jnp.where(rest >= 0, rest % major, k)
            l = jnp.where(rest >= 0, rest // major + 2, l)
        i, j = nearest(a, major, k), nearest(b, minor, l)
        return i * minor + j, i, j

    def take_part(slot, part, h, i, j):
        pltpu.make_async_copy(
            held.at[slot, h, :, spans[part]],
            held.at[slot, h, :, spans[part]],
            recv_sem.at[slot, part, h],
        ).wait()
        send_on(slot, part, h, i, j)

    ahead = minor == 2 and major == 4

    def take(place, h):
        slot, i, j = place
        for part in range(parts - 1):
            take_part(slot, part, h, i, j)
        passed = inner & (j != b) & ((i == 0) | (i == major - 1)) if ahead else jnp.bool_(False)

        @pl.when(jnp.logical_not(passed))
        def _():
            take_part(slot, parts - 1, h, i, j)

    shards = major * minor
    pairs = (shards - 2) // 2
    far = place_of(jnp.int32(shards - 2))

    def one_pair(turn, carry):
        pair, h = turn // kv_local, turn % kv_local
        here = [place_of(2 * pair + n) for n in range(2)]
        for place in here:
            take(place, h)
        if ahead:

            @pl.when(inner & (pair >= pairs - 2))
            def _():
                _, far_i, far_j = far
                i = jnp.where(pair == pairs - 1, far_i, major - 1 - far_i)
                take_part(i * minor + far_j, parts - 1, h, i, far_j)

        attend([place[0] for place in here], h, False)
        return carry

    lax.fori_loop(0, pairs * kv_local, one_pair, 0)

    def last_turn(h, carry):
        take(far, h)
        attend([far[0]], h, False, functools.partial(finish, h))
        return carry

    lax.fori_loop(0, kv_local, last_turn, 0)
    settle(me, a, b)

    def settle_one(n, carry):
        settle(*place_of(n))
        return carry

    lax.fori_loop(0, shards - 1, settle_one, 0)
    for turn in range(1, tp_size):
        for k in range(per_peer):
            for h in range(kv_local):
                swap(turn, k, h).wait()


def copy_out(attended, log_norm, attended_out, log_norm_out, sems):
    copies = [
        pltpu.make_async_copy(log_norm, log_norm_out, sems.at[0]),
        pltpu.make_async_copy(attended, attended_out, sems.at[1]),
    ]
    for copy in copies:
        copy.start()
    for copy in copies:
        copy.wait()


def body(tp_size, ctx_size, queries, rotated_key_rows, ordered_value_rows, block_order, live_blocks):
    tok_rows, own_columns = queries.shape
    kv_columns = rotated_key_rows.shape[1]
    kv_local = kv_columns // HEAD_SIZE
    heads_local = own_columns // HEAD_SIZE
    groups = heads_local // kv_local
    blocks_here = tok_rows // BLOCK_TOKENS
    width = groups * BLOCK_TOKENS
    major, minor = grid_of(ctx_size)
    cut = tok_rows // 2
    dims = (major, minor, tp_size, kv_local, groups, blocks_here, cut, live_blocks.shape[1])
    per_peer = blocks_here // tp_size
    whole = pl.BlockSpec(memory_space=pltpu.VMEM)
    apart = pl.BlockSpec(memory_space=pl.ANY)
    attended, log_norm = pl.pallas_call(
        functools.partial(kernel, dims),
        out_shape=(
            pltpu.VMEM((tok_rows // tp_size, own_columns * tp_size), jnp.bfloat16),
            pltpu.VMEM((heads_local, tok_rows), jnp.float32),
        ),
        in_specs=[apart] * 5,
        out_specs=(whole, whole),
        scratch_shapes=[
            pltpu.VMEM((ctx_size, kv_local, 2, tok_rows, HEAD_SIZE), jnp.bfloat16),
            pltpu.SMEM((1, block_order.shape[0]), jnp.int32),
            pltpu.SMEM(live_blocks.shape, jnp.int32),
            pltpu.VMEM((tok_rows, own_columns), jnp.bfloat16),
            pltpu.VMEM((blocks_here, kv_local, HEAD_SIZE, width), jnp.bfloat16),
            pltpu.VMEM((blocks_here, kv_local, HEAD_SIZE, width), jnp.float32),
            pltpu.VMEM((blocks_here, kv_local, 1, width), jnp.float32),
            pltpu.VMEM((blocks_here, kv_local, 1, width), jnp.float32),
            pltpu.VMEM((blocks_here, BLOCK_TOKENS, own_columns), jnp.bfloat16),
            pltpu.SMEM((ctx_size, blocks_here, blocks_here), jnp.float32),
            pltpu.VMEM((SLOTS, 2 * tok_rows, CHUNK), jnp.float32),
            pltpu.SemaphoreType.DMA((4, kv_local, 2)),
            pltpu.SemaphoreType.REGULAR((2,)),
            pltpu.SemaphoreType.DMA((ctx_size, 2, 4)),
            pltpu.SemaphoreType.DMA((ctx_size, 2, kv_local)),
            pltpu.SemaphoreType.DMA((tp_size - 1, per_peer, kv_local)),
            pltpu.SemaphoreType.DMA((tp_size - 1, per_peer, kv_local)),
        ],
        compiler_params=pltpu.CompilerParams(
            collective_id=0, has_side_effects=True, vmem_limit_bytes=VMEM_LIMIT
        ),
        name="gather_attend",
    )(queries, rotated_key_rows, ordered_value_rows, block_order.reshape(1, -1), live_blocks)
    return pl.pallas_call(
        copy_out,
        out_shape=(
            jax.ShapeDtypeStruct(attended.shape, attended.dtype),
            jax.ShapeDtypeStruct(log_norm.shape, log_norm.dtype),
        ),
        in_specs=[whole, whole],
        out_specs=(apart, apart),
        scratch_shapes=[pltpu.SemaphoreType.DMA((2,))],
        name="copy_out",
    )(
        pltpu.with_memory_space_constraint(attended, pltpu.VMEM),
        pltpu.with_memory_space_constraint(log_norm, pltpu.VMEM),
    )


def solution(mesh):
    placed = (
        P(("rep", "ctx"), "tp"),
        P(("rep", "ctx"), "tp"),
        P(("rep", "ctx"), "tp"),
        P("rep"),
        P("rep", None),
    )
    return jax.shard_map(
        functools.partial(body, mesh.shape["tp"], mesh.shape["ctx"]),
        mesh=mesh,
        in_specs=placed,
        out_specs=(P(("rep", "ctx", "tp"), None), P(("rep", "tp"), "ctx")),
        check_vma=False,
    )
```

```python
import functools
import math

import jax
import jax.numpy as jnp
from jax import lax
from jax.experimental import pallas as pl
from jax.experimental.pallas import tpu as pltpu
from jax.sharding import PartitionSpec as P

HEAD_SIZE = 128
BLOCK_TOKENS = 128
CHUNK = 256
STRIP = 32
SLOTS = 4
VMEM_LIMIT = 60 << 20
FAR = 1e30
HUGE = 3e38
MESH = pl.DeviceIdType.MESH


def grid_of(count):
    minor = max(d for d in range(1, math.isqrt(count) + 1) if count % d == 0)
    return count // minor, minor


def kernel(
    dims,
    queries,
    keys,
    values,
    block_order,
    live_blocks,
    attended,
    log_norm,
    held,
    order,
    live,
    raw_queries,
    turned_queries,
    total,
    peak,
    weight_sum,
    leaving,
    limits,
    scores,
    load_sem,
    answer,
    send_sem,
    recv_sem,
    swap_send,
    swap_recv,
):
    major, minor, tp_size, kv_local, groups, blocks_here, cut, slots_live = dims
    factor = HEAD_SIZE ** (-0.5)
    scale = factor * math.log2(math.e)
    width = groups * BLOCK_TOKENS
    rows = blocks_here * BLOCK_TOKENS
    spans = [pl.ds(0, cut), pl.ds(cut, rows - cut)]
    parts = len(spans)
    me = lax.axis_index("ctx")
    mine = lax.axis_index("tp")
    a, b = me // minor, me % minor
    per_peer = blocks_here // tp_size

    def real(q):
        return ((mine + 1) * per_peer + q) % blocks_here


    tables = [
        pltpu.make_async_copy(block_order, order, load_sem.at[0, 0, 0]),
        pltpu.make_async_copy(live_blocks, live, load_sem.at[1, 0, 0]),
    ]
    loads = [
        pltpu.make_async_copy(
            source.at[:, pl.ds(h * HEAD_SIZE, HEAD_SIZE)], held.at[me, h, kind], load_sem.at[3, h, kind]
        )
        for h in range(kv_local)
        for kind, source in enumerate((keys, values))
    ]
    load_queries = pltpu.make_async_copy(queries, raw_queries, load_sem.at[2, 0, 0])
    barrier = pltpu.get_barrier_semaphore()
    sides = (
        (a > 0, me - minor),
        (a < major - 1, me + minor),
        (b > 0, me - 1),
        (b < minor - 1, me + 1),
    )
    lower, upper = (0, 2), (1, 3)
    for side in upper:
        there, who = sides[side]

        @pl.when(there)
        def _(who=who):
            pl.semaphore_signal(barrier, inc=1, device_id={"ctx": who}, device_id_type=MESH)

    for turn in range(1, tp_size):
        peer = (mine + turn) % tp_size
        pl.semaphore_signal(barrier, inc=1, device_id={"tp": peer}, device_id_type=MESH)
    for load in loads:
        load.start()
    expected = jnp.int32(tp_size - 1)
    for side in lower:
        expected = expected + sides[side][0].astype(jnp.int32)
    pl.semaphore_wait(barrier, expected)
    for side in lower:
        there, who = sides[side]

        @pl.when(there)
        def _(who=who, side=side):
            pl.semaphore_signal(
                answer.at[side // 2], inc=1, device_id={"ctx": who}, device_id_type=MESH
            )

    def onward(part, i, j):
        column_first = j == b
        row_first = (i == 0) | (i == major - 1) if part == parts - 1 else jnp.bool_(False)
        along = column_first | row_first
        across = (i == a) | jnp.logical_not(row_first)
        return (
            (i >= a) & (a > 0) & along,
            (i <= a) & (a < major - 1) & along,
            (j >= b) & (b > 0) & across,
            (j <= b) & (b < minor - 1) & across,
        )

    def send_on(slot, part, h, i, j, to=range(4)):
        wanted = onward(part, i, j)
        for side in to:

            @pl.when(wanted[side])
            def _(side=side):
                pltpu.make_async_remote_copy(
                    src_ref=held.at[slot, h, :, spans[part]],
                    dst_ref=held.at[slot, h, :, spans[part]],
                    send_sem=send_sem.at[slot, part, side],
                    recv_sem=recv_sem.at[slot, part, h],
                    device_id={"ctx": sides[side][1]},
                    device_id_type=MESH,
                ).start()

    def send_own(part, h, to):
        wanted = onward(part, a, b)
        for side in to:

            @pl.when(wanted[side])
            def _(side=side):
                for kind, source in enumerate((keys, values)):
                    pltpu.make_async_remote_copy(
                        src_ref=source.at[spans[part], pl.ds(h * HEAD_SIZE, HEAD_SIZE)],
                        dst_ref=held.at[me, h, kind, spans[part]],
                        send_sem=send_sem.at[me, part, side],
                        recv_sem=recv_sem.at[me, part, h],
                        device_id={"ctx": sides[side][1]},
                        device_id_type=MESH,
                    ).start()

    def settle(slot, i, j):
        for part in range(parts):
            for side, wanted in enumerate(onward(part, i, j)):

                @pl.when(wanted)
                def _(part=part, side=side):
                    pltpu.make_async_copy(
                        held.at[slot, :, :, spans[part]],
                        held.at[slot, :, :, spans[part]],
                        send_sem.at[slot, part, side],
                    ).wait()

    def find_limits(slot, carry):
        for q in range(blocks_here):
            my_seq = order[0, me * blocks_here + real(q)]
            found = [jnp.bool_(False)] * blocks_here
            names = [order[0, slot * blocks_here + kb] for kb in range(blocks_here)]
            for entry in range(slots_live):
                listed = live[my_seq, entry]
                found = [f | (listed == name) for f, name in zip(found, names)]
            for kb in range(blocks_here):
                limits[slot, q, kb] = jnp.where(found[kb], HUGE, -FAR)
        return carry

    def attend(slots, h, first, after=None):
        keys_here = [held[slot, h, 0] for slot in slots]
        turned_values = jnp.concatenate([jnp.transpose(held[slot, h, 1]) for slot in slots], axis=1)
        ones = jnp.ones((16, turned_values.shape[1]), turned_values.dtype)
        turned_values = jnp.concatenate([turned_values, ones], axis=0)
        units = [(q, start) for q in range(blocks_here) for start in range(0, width, CHUNK)]
        blocks = [(n, slot, kb) for n, slot in enumerate(slots) for kb in range(blocks_here)]

        def score(u):
            q, start = units[u]
            turned_here = turned_queries[q, h, :, pl.ds(start, CHUNK)]
            parts = [
                jnp.dot(k, turned_here, preferred_element_type=jnp.float32) for k in keys_here
            ]
            tops = []
            for n, slot, kb in blocks:
                block = parts[n][kb * BLOCK_TOKENS : (kb + 1) * BLOCK_TOKENS]
                if first:
                    key_at = lax.broadcasted_iota(jnp.int32, block.shape, 0)
                    row_at = lax.broadcasted_iota(jnp.int32, block.shape, 1) % BLOCK_TOKENS
                    row_at = row_at + (real(q) != kb).astype(jnp.int32) * BLOCK_TOKENS
                    block = jnp.where(key_at <= row_at, block, -FAR)
                at = n * rows + kb * BLOCK_TOKENS
                scores[u % SLOTS, pl.ds(at, BLOCK_TOKENS), :] = block
                tops.append(jnp.max(block, axis=0, keepdims=True))
            return tops

        def absorb(u, tops):
            q, start = units[u]
            lanes = pl.ds(start, CHUNK)
            new_peak = None
            for (n, slot, kb), top in zip(blocks, tops):
                top = jnp.minimum(top, limits[slot, q, kb])
                new_peak = top if new_peak is None else jnp.maximum(new_peak, top)
            if not first:
                old_peak = peak[q, h, :, lanes]
                new_peak = jnp.maximum(new_peak, old_peak)
            peak[q, h, :, lanes] = new_peak
            level = new_peak * scale
            added = None
            low = []
            for n, slot, kb in blocks:
                floor = jnp.maximum(level, -limits[slot, q, kb])
                start_at = n * rows + kb * BLOCK_TOKENS
                for at in range(start_at, start_at + BLOCK_TOKENS, STRIP):
                    w = jnp.exp2(scores[u % SLOTS, pl.ds(at, STRIP), :] * scale - floor)
                    low.append(w.astype(jnp.bfloat16))
            product = jnp.dot(
                turned_values,
                jnp.concatenate(low, axis=0),
                preferred_element_type=jnp.float32,
            )
            added, product = product[HEAD_SIZE : HEAD_SIZE + 1], product[:HEAD_SIZE]
            if first:
                weight_sum[q, h, :, lanes] = added
                total[q, h, :, lanes] = product
            else:
                fade = jnp.exp2((old_peak - new_peak) * scale)
                weight_sum[q, h, :, lanes] = (
                    weight_sum[q, h, :, lanes] * fade + added
                )
                total[q, h, :, lanes] = total[q, h, :, lanes] * fade + product

        waiting = [score(u) for u in range(SLOTS - 1)]
        for u in range(len(units)):
            if u + SLOTS - 1 < len(units):
                waiting.append(score(u + SLOTS - 1))
            absorb(u, waiting[u])
            if after is not None and (u + 1) % (len(units) // blocks_here) == 0:
                after(units[u][0])

    wide = kv_local * width

    def swap(turn, k, h):
        peer = (mine + turn) % tp_size
        source = pl.ds(pl.multiple_of(h * width, HEAD_SIZE), width)
        target = pl.ds(pl.multiple_of(mine * wide + h * width, HEAD_SIZE), width)
        return pltpu.make_async_remote_copy(
            src_ref=leaving.at[(turn - 1) * per_peer + k, :, source],
            dst_ref=attended.at[pl.ds(k * BLOCK_TOKENS, BLOCK_TOKENS), target],
            send_sem=swap_send.at[turn - 1, k, h],
            recv_sem=swap_recv.at[turn - 1, k, h],
            device_id={"tp": peer},
            device_id_type=MESH,
        )

    def finish(h, q):
        turn, k = 1 + q // per_peer, q % per_peer
        at = pl.ds(pl.multiple_of(real(q) * BLOCK_TOKENS, BLOCK_TOKENS), BLOCK_TOKENS)
        norms = []
        for g in range(groups):
            head = h * groups + g
            lanes = pl.ds(g * BLOCK_TOKENS, BLOCK_TOKENS)
            bottom = weight_sum[q, h, :, lanes]
            normed = total[q, h, :, lanes] * (1.0 / bottom)
            tile = jnp.transpose(normed.astype(jnp.bfloat16))
            if turn < tp_size:
                to = pl.multiple_of(head * HEAD_SIZE, HEAD_SIZE)
                leaving[q, :, pl.ds(to, HEAD_SIZE)] = tile
            else:
                to = pl.multiple_of(mine * wide + head * HEAD_SIZE, HEAD_SIZE)
                attended[pl.ds(k * BLOCK_TOKENS, BLOCK_TOKENS), pl.ds(to, HEAD_SIZE)] = tile
            norms.append(peak[q, h, :, lanes] * factor + jnp.log(bottom))
        heads = pl.ds(pl.multiple_of(h * groups, groups), groups)
        log_norm[heads, at] = jnp.concatenate(norms, axis=0)
        if turn < tp_size:
            swap(turn, k, h).start()

    for part in range(parts):
        send_own(part, 0, lower)
    for load in [load_queries] + tables:
        load.start()
    for load in loads:
        load.wait()
    for h in range(1, kv_local):
        for part in range(parts):
            send_on(me, part, h, a, b, lower)
    for side in upper:

        @pl.when(sides[side][0])
        def _(side=side):
            pl.semaphore_wait(answer.at[side // 2], 1)

    for h in range(kv_local):
        for part in range(parts):
            send_on(me, part, h, a, b, upper)
    for load in [load_queries] + tables:
        load.wait()

    def turn_block(q, carry):
        at = pl.ds(pl.multiple_of(real(q) * BLOCK_TOKENS, BLOCK_TOKENS), BLOCK_TOKENS)
        for h in range(kv_local):
            for g in range(groups):
                head = h * groups + g
                turned_queries[q, h, :, pl.ds(g * BLOCK_TOKENS, BLOCK_TOKENS)] = jnp.transpose(
                    raw_queries[at, pl.ds(head * HEAD_SIZE, HEAD_SIZE)]
                )
        return carry

    lax.fori_loop(0, blocks_here, turn_block, 0)
    lax.fori_loop(me, me + 1, find_limits, 0)

    def attend_own(h, carry):
        attend([me], h, True)
        return carry

    lax.fori_loop(0, kv_local, attend_own, 0)
    lax.fori_loop(0, major * minor, find_limits, 0)

    def nearest(x, n, k):
        both = jnp.minimum(x, n - 1 - x)
        away = 1 - 2 * (2 * x > n - 1).astype(jnp.int32)
        paired = ((k + 1) // 2) * (2 * (k % 2) - 1)
        return x + away * jnp.where(k <= 2 * both, paired, k - both)

    inner = (a > 0) & (a < major - 1)
    lag = 1 + inner.astype(jnp.int32)
    both = 2 * (major - 1 - lag)

    def place_of(n):
        later = n - lag
        column = (n < lag) | ((later < both) & (later % 2 == 1))
        k = jnp.where(later < both, later // 2, later - both // 2)
        k = jnp.where(n < lag, n + 1, k + column * (lag + 1))
        l = jnp.where(column, 0, 1)
        if minor > 2:
            rest = n - (2 * major - 1)
            k = jnp.where(rest >= 0, rest % major, k)
            l = jnp.where(rest >= 0, rest // major + 2, l)
        i, j = nearest(a, major, k), nearest(b, minor, l)
        return i * minor + j, i, j

    def take_part(slot, part, h, i, j):
        pltpu.make_async_copy(
            held.at[slot, h, :, spans[part]],
            held.at[slot, h, :, spans[part]],
            recv_sem.at[slot, part, h],
        ).wait()
        send_on(slot, part, h, i, j)

    ahead = minor == 2 and major == 4

    def take(place, h):
        slot, i, j = place
        for part in range(parts - 1):
            take_part(slot, part, h, i, j)
        passed = inner & (j != b) & ((i == 0) | (i == major - 1)) if ahead else jnp.bool_(False)

        @pl.when(jnp.logical_not(passed))
        def _():
            take_part(slot, parts - 1, h, i, j)

    shards = major * minor
    pairs = (shards - 2) // 2
    far = place_of(jnp.int32(shards - 2))

    def one_pair(turn, carry):
        pair, h = turn // kv_local, turn % kv_local
        here = [place_of(2 * pair + n) for n in range(2)]
        for place in here:
            take(place, h)
        if ahead:

            @pl.when(inner & (pair >= pairs - 2))
            def _():
                _, far_i, far_j = far
                i = jnp.where(pair == pairs - 1, far_i, major - 1 - far_i)
                take_part(i * minor + far_j, parts - 1, h, i, far_j)

        attend([place[0] for place in here], h, False)
        return carry

    lax.fori_loop(0, pairs * kv_local, one_pair, 0)

    def last_turn(h, carry):
        take(far, h)
        attend([far[0]], h, False, functools.partial(finish, h))
        return carry

    lax.fori_loop(0, kv_local, last_turn, 0)
    settle(me, a, b)

    def settle_one(n, carry):
        settle(*place_of(n))
        return carry

    lax.fori_loop(0, shards - 1, settle_one, 0)
    for turn in range(1, tp_size):
        for k in range(per_peer):
            for h in range(kv_local):
                swap(turn, k, h).wait()


def copy_out(attended, log_norm, attended_out, log_norm_out, sems):
    copies = [
        pltpu.make_async_copy(log_norm, log_norm_out, sems.at[0]),
        pltpu.make_async_copy(attended, attended_out, sems.at[1]),
    ]
    for copy in copies:
        copy.start()
    for copy in copies:
        copy.wait()


def body(tp_size, ctx_size, queries, rotated_key_rows, ordered_value_rows, block_order, live_blocks):
    tok_rows, own_columns = queries.shape
    kv_columns = rotated_key_rows.shape[1]
    kv_local = kv_columns // HEAD_SIZE
    heads_local = own_columns // HEAD_SIZE
    groups = heads_local // kv_local
    blocks_here = tok_rows // BLOCK_TOKENS
    width = groups * BLOCK_TOKENS
    major, minor = grid_of(ctx_size)
    cut = tok_rows // 2
    dims = (major, minor, tp_size, kv_local, groups, blocks_here, cut, live_blocks.shape[1])
    per_peer = blocks_here // tp_size
    whole = pl.BlockSpec(memory_space=pltpu.VMEM)
    apart = pl.BlockSpec(memory_space=pl.ANY)
    attended, log_norm = pl.pallas_call(
        functools.partial(kernel, dims),
        out_shape=(
            pltpu.VMEM((tok_rows // tp_size, own_columns * tp_size), jnp.bfloat16),
            pltpu.VMEM((heads_local, tok_rows), jnp.float32),
        ),
        in_specs=[apart] * 5,
        out_specs=(whole, whole),
        scratch_shapes=[
            pltpu.VMEM((ctx_size, kv_local, 2, tok_rows, HEAD_SIZE), jnp.bfloat16),
            pltpu.SMEM((1, block_order.shape[0]), jnp.int32),
            pltpu.SMEM(live_blocks.shape, jnp.int32),
            pltpu.VMEM((tok_rows, own_columns), jnp.bfloat16),
            pltpu.VMEM((blocks_here, kv_local, HEAD_SIZE, width), jnp.bfloat16),
            pltpu.VMEM((blocks_here, kv_local, HEAD_SIZE, width), jnp.float32),
            pltpu.VMEM((blocks_here, kv_local, 1, width), jnp.float32),
            pltpu.VMEM((blocks_here, kv_local, 1, width), jnp.float32),
            pltpu.VMEM((blocks_here, BLOCK_TOKENS, own_columns), jnp.bfloat16),
            pltpu.SMEM((ctx_size, blocks_here, blocks_here), jnp.float32),
            pltpu.VMEM((SLOTS, 2 * tok_rows, CHUNK), jnp.float32),
            pltpu.SemaphoreType.DMA((4, kv_local, 2)),
            pltpu.SemaphoreType.REGULAR((2,)),
            pltpu.SemaphoreType.DMA((ctx_size, 2, 4)),
            pltpu.SemaphoreType.DMA((ctx_size, 2, kv_local)),
            pltpu.SemaphoreType.DMA((tp_size - 1, per_peer, kv_local)),
            pltpu.SemaphoreType.DMA((tp_size - 1, per_peer, kv_local)),
        ],
        compiler_params=pltpu.CompilerParams(
            collective_id=0, has_side_effects=True, vmem_limit_bytes=VMEM_LIMIT
        ),
        name="gather_attend",
    )(queries, rotated_key_rows, ordered_value_rows, block_order.reshape(1, -1), live_blocks)
    return pl.pallas_call(
        copy_out,
        out_shape=(
            jax.ShapeDtypeStruct(attended.shape, attended.dtype),
            jax.ShapeDtypeStruct(log_norm.shape, log_norm.dtype),
        ),
        in_specs=[whole, whole],
        out_specs=(apart, apart),
        scratch_shapes=[pltpu.SemaphoreType.DMA((2,))],
        name="copy_out",
    )(
        pltpu.with_memory_space_constraint(attended, pltpu.VMEM),
        pltpu.with_memory_space_constraint(log_norm, pltpu.VMEM),
    )


def solution(mesh):
    placed = (
        P(("rep", "ctx"), "tp"),
        P(("rep", "ctx"), "tp"),
        P(("rep", "ctx"), "tp"),
        P("rep"),
        P("rep", None),
    )
    return jax.shard_map(
        functools.partial(body, mesh.shape["tp"], mesh.shape["ctx"]),
        mesh=mesh,
        in_specs=placed,
        out_specs=(P(("rep", "ctx", "tp"), None), P(("rep", "tp"), "ctx")),
        check_vma=False,
    )
```
